256 devices in a mesh: pop: 32 (over x_lo, z, core), tp: 8 (over x_hi, y).
Axes of the slice: x: 4 (x_hi: 2, x_lo: 2; x = x_hi * 2 + x_lo), y: 4, z: 8, core: 2. Of those that a mesh axis runs over, the one named last changes fastest.
Arguments:
- hidden: bfloat16 [2048, 5120], P('pop', 'tp'), may hold values from -24 to 24
- norm_gain: float32 [5120], P('tp'), may hold values from 0.25 to 1.75
- right_factors: bfloat16 [5120, 128], P('tp'), may hold values from -0.078125 to 0.078125
- left_factors: bfloat16 [77824, 128], P(('pop', 'tp')), may hold values from -4 to 4
- targets: int32 [2048], replicated, may hold values from 0 to 77823
- master: float32 [77824, 5120], P(('pop', 'tp')), may hold values from -0.2934839 to 0.2934839
Outputs:
- member_loglik: float32 [64], replicated
- new_master: float32 [77824, 5120], P(('pop', 'tp'))
The draws below stay inside these ranges and needn't reach their ends.
All inputs are finite; a program needn't handle non-finite values.
Results may differ from the reference program's by a relative error of at most 0.0026.
The reference program's roundings to bfloat16 on the way (of `normed`, `lowrank`, `head` and `scaled_left`) count: a program that leaves them out, or rounds other values in their place, can miss the bound.
Values may be sent and summed in bfloat16 or wider, within the bound.
A program may use at most 128 MiB of HBM per device.

```python
import jax
import jax.numpy as jnp
from jax import lax

D = 5120
VOC_DEV = 304
RANK = 4
SEQ = 32
PAIRS = 32
MEMBERS = 64
ALL_TOK = 2048
FACT = 128
VOCAB = 77824


SPREAD_LOGIT = 3.5


ALIGN_LEVELS = (480.0, 110.0, 400.0, 160.0, 330.0, 220.0, 270.0, 450.0)


JITTER_LEVELS = (0.05, 0.2, 0.5, 1.0, 0.1, 0.3, 0.7, 0.05)


def base_rows(key, row_id):
    return jax.random.normal(jax.random.fold_in(jax.random.fold_in(key, 11), row_id), (D,), jnp.float32)


def drawn_pattern(key, row_id):
    return jnp.clip(base_rows(key, row_id), -3.0, 3.0)


def drawn_rows(key):
    order = jax.random.permutation(jax.random.fold_in(key, 41), VOCAB).astype(jnp.int32)
    return (order[:8], order[8:16])


def drawn_tokens(key):
    order = jax.random.permutation(jax.random.fold_in(key, 43), ALL_TOK).astype(jnp.int32)
    return order[:8]


def draw_master(key, part):
    spread = SPREAD_LOGIT / jnp.sqrt(jnp.float32(D))
    levels = jnp.array(ALIGN_LEVELS, jnp.float32)
    strong = levels / jnp.float32(D)
    row_ids = jnp.arange(VOCAB, dtype=jnp.int32)
    matrix = jax.vmap(lambda row_id: jnp.clip(base_rows(key, row_id), -6.0, 6.0) * spread)(row_ids)
    leads, pairs = drawn_rows(key)
    peaked = jax.vmap(lambda row_id: drawn_pattern(key, row_id))(leads) * strong[:, None]
    jitter = jnp.clip(jax.random.normal(jax.random.fold_in(key, 13), (8, D), jnp.float32), -6.0, 6.0) * (0.004 * strong[:, None])
    factor = 1.0 - 2.0 / levels
    matrix = matrix.at[leads].set(peaked)
    matrix = matrix.at[pairs].set(factor[:, None] * peaked + jitter)
    return matrix


def draw_hidden(key, part):
    matrix = jnp.clip(jax.random.normal(jax.random.fold_in(key, 23), (ALL_TOK, D), jnp.float32), -6.0, 6.0)
    leads, pairs = drawn_rows(key)
    token_rows = drawn_tokens(key)
    patterns = jax.vmap(lambda row_id: drawn_pattern(key, row_id))(leads)
    jitter_scale = jnp.array(JITTER_LEVELS, jnp.float32)
    jitter = jnp.clip(jax.random.normal(jax.random.fold_in(key, 31), (8, D), jnp.float32), -6.0, 6.0) * jitter_scale[:, None]
    matrix = matrix.at[token_rows].set(patterns + jitter)
    return matrix.astype(jnp.bfloat16)


def place_ends(entries, own_key, least, top_value):
    longest = entries.shape.index(max(entries.shape))
    spots = []
    for shift in (0, 1):
        where = [jax.random.randint(jax.random.fold_in(own_key, axis), (), 0, length) for axis, length in enumerate(entries.shape)]
        where[longest] = (where[longest] + shift) % entries.shape[longest]
        spots.append(tuple(where))
    return entries.at[spots[0]].set(least).at[spots[1]].set(top_value)


def level_of(key, extent, pieces, smallest, largest):
    gain, own = 1.0, jax.random.fold_in(key, 6)
    for dim, parts in pieces:
        steps = jnp.exp(jax.random.uniform(jax.random.fold_in(own, dim), (parts,), jnp.float32, smallest / len(pieces), largest / len(pieces)))
        gain = gain * jnp.repeat(steps, extent[dim] // parts).reshape([-1 if axis == dim else 1 for axis in range(len(extent))])
    return gain


def scatter_about(own_key, shape, scale, most, cuts=(), kind=jnp.bfloat16):
    level = level_of(own_key, shape, cuts, -0.22, 0.18) if cuts else 1.0
    drawn = jax.random.normal(own_key, shape, jnp.float32) * scale * level
    return jnp.minimum(jnp.maximum(drawn, -most), most).astype(kind)


def setup_inputs(seed: int = 0) -> dict:
    key_list = jax.random.split(jax.random.key(seed), 7)
    hidden = draw_hidden(jax.random.fold_in(key_list[6], 71), 0)
    norm_gain = jnp.clip(1.0 + 0.15 * jax.random.normal(key_list[1], (D,), jnp.float32), 0.25, 1.75)
    right_factors = scatter_about(key_list[2], (D, FACT), D ** -0.5, 0.078125, ((0, 8),))
    left_factors = scatter_about(key_list[3], (VOCAB, FACT), 1.0, 4.0, ((0, 256),))
    targets = place_ends(jax.random.randint(key_list[4], (ALL_TOK,), 0, VOCAB), jax.random.fold_in(key_list[4], 1), 0, VOCAB - 1).astype(jnp.int32)
    master = draw_master(jax.random.fold_in(key_list[6], 71), 0)
    return {"hidden": hidden, "norm_gain": norm_gain, "right_factors": right_factors, "left_factors": left_factors, "targets": targets, "master": master}


NORM_EPS = 1e-06
SIGMA_NOISE = 0.25
LEARN_RATE = 0.5

def contract(left, right):
    return lax.dot_general(left, right, (((1,), (1,)), ((), ())), preferred_element_type=jnp.float32)

def reference(hidden, norm_gain, right_factors, left_factors, targets, master):
    values = hidden.astype(jnp.float32)
    squares = lax.optimization_barrier(jnp.sum(values * values, axis=1))
    row_scale = lax.rsqrt(squares / D + NORM_EPS)
    normed = (values * row_scale[:, None] * norm_gain[None, :]).astype(jnp.bfloat16)
    grouped = normed.reshape(PAIRS, 2 * SEQ, D).astype(jnp.float32)
    columns = right_factors.astype(jnp.float32).reshape(D, PAIRS, RANK)
    projection = jnp.einsum('prd,dpk->prk', grouped, columns)
    member_sign = jnp.where(jnp.arange(2 * SEQ) < SEQ, SIGMA_NOISE, -SIGMA_NOISE).astype(jnp.float32)
    scaled = projection * member_sign[None, :, None]
    selector = jnp.eye(PAIRS, dtype=jnp.float32)
    lowrank = (scaled[:, :, None, :] * selector[:, None, :, None]).reshape(ALL_TOK, FACT).astype(jnp.bfloat16)
    head = master.astype(jnp.bfloat16)
    columns_ids = jnp.arange(VOC_DEV, dtype=jnp.int32)

    def visit(carry, block_id):
        run_max, run_sum, run_target = carry
        start = (block_id * VOC_DEV).astype(jnp.int32)
        weights = lax.dynamic_slice_in_dim(head, start, VOC_DEV, 0)
        factors = lax.dynamic_slice_in_dim(left_factors, start, VOC_DEV, 0)
        logits = contract(normed, weights) + contract(lowrank, factors)
        block_max = lax.optimization_barrier(jnp.max(logits, axis=1))
        block_sum = lax.optimization_barrier(jnp.sum(jnp.exp(logits - block_max[:, None]), axis=1))
        picked = lax.optimization_barrier(jnp.sum(jnp.where(start + columns_ids[None, :] == targets[:, None], logits, 0.0), axis=1))
        joined = jnp.maximum(run_max, block_max)
        merged = run_sum * jnp.exp(run_max - joined) + block_sum * jnp.exp(block_max - joined)
        return ((joined, merged, run_target + picked), None)
    start_carry = (jnp.full((ALL_TOK,), -jnp.inf, jnp.float32), jnp.zeros((ALL_TOK,), jnp.float32), jnp.zeros((ALL_TOK,), jnp.float32))
    final, unused = lax.scan(visit, start_carry, jnp.arange(VOCAB // VOC_DEV, dtype=jnp.int32))
    row_max, row_sum, target_logit = final
    logprob = target_logit - row_max - jnp.log(row_sum)
    member_loglik = lax.optimization_barrier(jnp.mean(logprob.reshape(MEMBERS, SEQ), axis=1))
    fitness = member_loglik[0::2] - member_loglik[1::2]
    weight_cols = jnp.repeat(fitness, RANK)
    scaled_left = (left_factors.astype(jnp.float32) * weight_cols[None, :]).astype(jnp.bfloat16)
    update = contract(scaled_left, right_factors)
    new_master = master + LEARN_RATE * update
    return (member_loglik, new_master)
```

```python
import jax
import jax.numpy as jnp
from jax import lax
from jax.experimental import pallas as pl
from jax.experimental.pallas import tpu as pltpu
from jax.sharding import PartitionSpec as P

D = 5120
RANK = 4
NORM_EPS = 1e-06
SIGMA_NOISE = 0.25
LEARN_RATE = 0.5
NX, NY, NZ = 4, 4, 8
ROWS = 64
FEAT = 640
WA, WB = 128, 256
VOC = 304
FACT = 128
AUG = VOC + FACT
F32, BF16 = jnp.float32, jnp.bfloat16
MESH_ID = pl.DeviceIdType.MESH
NT = (((1,), (1,)), ((), ()))


class Ids:
    def __init__(self):
        self.table = {}

    def __call__(self, *key):
        return self.table.setdefault(key, len(self.table))


def message_names():
    ids = Ids()
    for d in range(1, 8):
        ids("sq", d)
    for d in range(1, 4):
        for kind in ("Rt", "B1", "C1", "A1", "A2"):
            ids(kind, d)
    ids("Rx")
    ids("Rd")
    for part in "ABC":
        for s in range(1, 5):
            ids("z", part, "up", s)
            if s < 4:
                ids("z", part, "dn", s)
    for k in range(8):
        for part in "BC":
            for way in ("up", "dn", "opp"):
                ids("last", part, k, way)
        for part in "ABC":
            ids("core", part, k)
    for d in range(1, 16):
        for stage in (1, 2, 3):
            ids("stat", stage, d)
    return ids


IDS = message_names()
N_MSG = len(IDS.table)


def combine(stats):
    top = stats[:, 0, :]
    best = jnp.max(top, axis=0, keepdims=True)
    total = jnp.sum(stats[:, 1, :] * jnp.exp(top - best), axis=0, keepdims=True)
    target = jnp.sum(stats[:, 2, :], axis=0, keepdims=True)
    return best, total, target


def gather_kernel(
    hid_ref, gain_ref, right_ref, left_ref, tgt_ref, master_ref,
    out_ref, rt_out_ref,
    buf_a, buf_b, buf_c, head_a, head_b, head_c, rt, stage, sq, st, r1, r2, r3,
    ssem, rsem, lsem,
):
    pop, tp = lax.axis_index("pop"), lax.axis_index("tp")
    c = lax.rem(pop, 2)
    z = lax.rem(lax.div(pop, 2), NZ)
    x_lo = lax.div(pop, 2 * NZ)
    x_hi = lax.div(tp, NY)
    y = lax.rem(tp, NY)
    x = x_hi * 2 + x_lo
    sib = 1 - c
    sgn = 1 - 2 * c

    def dev(xx, yy, zz, cc):
        return ((lax.rem(xx, 2) * NZ + zz) * 2 + cc, lax.div(xx, 2) * NY + yy)

    def off(v, k, n):
        return lax.rem(v + k * sgn + n, n)

    def plus(v, k, n):
        return lax.rem(v + k + n, n)

    sent = []

    def send(key, src, dst, device):
        i = IDS(*key)
        copy = pltpu.make_async_remote_copy(
            src_ref=src, dst_ref=dst, send_sem=ssem.at[i], recv_sem=rsem.at[i],
            device_id=device, device_id_type=MESH_ID,
        )
        copy.start()
        sent.append(copy)

    def recv(key, dst, device):
        i = IDS(*key)
        pltpu.make_async_remote_copy(
            src_ref=dst, dst_ref=dst, send_sem=ssem.at[i], recv_sem=rsem.at[i],
            device_id=device, device_id_type=MESH_ID,
        ).wait_recv()

    load = pltpu.make_async_copy(master_ref, stage, lsem.at[0])
    load.start()

    blk = x_lo * NZ + z
    quad = c * 8 + tp

    def blk_dev(b):
        return dev(x_hi * 2 + lax.div(b, NZ), y, lax.rem(b, NZ), c)

    def quad_dev(q):
        t = lax.rem(q, 8)
        return dev(lax.div(t, NY) * 2 + x_lo, lax.rem(t, NY), z, lax.div(q, 8))

    mirror = dev(3 - x, y, z, c)

    barrier = pltpu.get_barrier_semaphore()
    for d in range(1, 16):
        pl.semaphore_signal(barrier, inc=1, device_id=blk_dev(plus(blk, d, 16)), device_id_type=MESH_ID)
        pl.semaphore_signal(barrier, inc=1, device_id=quad_dev(plus(quad, d, 16)), device_id_type=MESH_ID)
    pl.semaphore_signal(barrier, inc=1, device_id=mirror, device_id_type=MESH_ID)

    values = hid_ref[...].astype(F32)
    squares = values * values
    folded = squares[:, 0:128]
    for j in range(1, FEAT // 128):
        folded = folded + squares[:, j * 128:(j + 1) * 128]
    folded = jnp.concatenate([folded, jnp.zeros((128 - ROWS, 128), F32)], axis=0)
    row_sq = jnp.sum(folded.T, axis=0, keepdims=True)
    sq[pl.ds(tp, 1)] = jnp.broadcast_to(row_sq, (8, 128))[None]
    for j in range(FEAT // 128):
        block_t = right_ref[j * 128:(j + 1) * 128, :].astype(F32).T.astype(BF16)
        rt[c, pl.ds(tp, 1), :, j * 128:(j + 1) * 128] = jnp.where(c == 0, block_t[:64], block_t[64:])[None]

    pl.semaphore_wait(barrier, 31)

    for d in range(1, 8):
        t = plus(tp, d, 8)
        send(("sq", d), sq.at[tp], sq.at[tp], dev(lax.div(t, NY) * 2 + x_lo, lax.rem(t, NY), z, c))
    for d in range(1, 4):
        send(("Rt", d), rt.at[c, tp], rt.at[c, tp], dev(x, plus(y, d, NY), z, c))
    for d in range(1, 8):
        t = plus(tp, -d, 8)
        recv(("sq", d), sq.at[t], dev(lax.div(t, NY) * 2 + x_lo, lax.rem(t, NY), z, c))

    row_scale = lax.rsqrt(jnp.sum(sq[:, 0, :], axis=0, keepdims=True) / D + NORM_EPS)
    scale = jnp.broadcast_to(row_scale, (128, 128)).T[:ROWS, :]
    scaled = jnp.concatenate(
        [values[:, j * 128:(j + 1) * 128] * scale for j in range(FEAT // 128)], axis=1
    )
    normed = (scaled * gain_ref[...]).astype(BF16)
    buf_b[z, c, y, x] = normed[:, WA:WA + WB]
    buf_c[z, c, x, y] = normed[:, WA + WB:]
    buf_a[z, c, y, x] = normed[:, :WA]

    for d in (1, 3, 2):
        send(("B1", d), buf_b.at[z, c, y, x], buf_b.at[z, c, y, x], dev(plus(x, d, NX), y, z, c))
        send(("C1", d), buf_c.at[z, c, x, y], buf_c.at[z, c, x, y], dev(x, plus(y, d, NY), z, c))
    for d in (1, 3, 2):
        send(("A1", d), buf_a.at[z, c, y, x], buf_a.at[z, c, y, x], dev(plus(x, d, NX), y, z, c))

    def z_dev(k):
        return dev(x, y, off(z, k, NZ), c)

    def y_dev(k):
        return dev(x, off(y, k, NY), z, c)

    def x_dev(k):
        return dev(off(x, k, NX), y, z, c)

    def blk_a(zz):
        return buf_a.at[zz, c]

    def blk_b(zz, yy):
        return buf_b.at[zz, c, yy]

    def blk_c(zz, xx):
        return buf_c.at[zz, c, xx]

    def z_blk(part, zz):
        return {"A": lambda: blk_a(zz), "B": lambda: blk_b(zz, y), "C": lambda: blk_c(zz, x)}[part]()

    slots = {0: [(0, "own", 0)], 4: [(7, "up", 4)]}
    for s in (1, 2, 3):
        slots[s] = [(2 * s - 1, "up", s), (2 * s, "dn", s)]

    def slot_z(way, s, orient=1):
        return off(z, -orient * s if way == "up" else orient * s, NZ)

    def last_send(part, k, zz):
        if part == "B":
            send(("last", part, k, "up"), blk_b(zz, y), blk_b(zz, y), y_dev(1))
            send(("last", part, k, "dn"), blk_b(zz, y), blk_b(zz, y), y_dev(-1))
        else:
            send(("last", part, k, "up"), blk_c(zz, x), blk_c(zz, x), x_dev(1))
            send(("last", part, k, "dn"), blk_c(zz, x), blk_c(zz, x), x_dev(-1))

    def z_start(part):
        send(("z", part, "up", 1), z_blk(part, z), z_blk(part, z), z_dev(1))
        send(("z", part, "dn", 1), z_blk(part, z), z_blk(part, z), z_dev(-1))

    def z_recv(s):
        for part in ("B", "C", "A"):
            for k, way, _ in slots[s]:
                zz = slot_z(way, s)
                step = 1 if way == "up" else -1
                recv(("z", part, way, s), z_blk(part, zz), z_dev(-step))
                if s < (4 if way == "up" else 3):
                    send(("z", part, way, s + 1), z_blk(part, zz), z_blk(part, zz), z_dev(step))
                if part != "A":
                    last_send(part, k, zz)

    def y_recv(s):
        for k, way, _ in slots[s]:
            zz = slot_z(way, s)
            below = blk_b(zz, off(y, -1, NY))
            recv(("last", "B", k, "up"), below, y_dev(-1))
            send(("last", "B", k, "opp"), below, below, y_dev(1))
            below = blk_c(zz, off(x, -1, NX))
            recv(("last", "C", k, "up"), below, x_dev(-1))
            send(("last", "C", k, "opp"), below, below, x_dev(1))

    def core_send(part, k, ref, zz):
        send(("core", part, k), ref.at[zz, c], ref.at[zz, c], dev(x, y, z, sib))

    def o_recv(s):
        for k, way, _ in slots[s]:
            zz = slot_z(way, s)
            core_send("A", k, buf_a, zz)
            recv(("last", "B", k, "dn"), blk_b(zz, off(y, 1, NY)), y_dev(1))
            recv(("last", "B", k, "opp"), blk_b(zz, off(y, 2, NY)), y_dev(-1))
            core_send("B", k, buf_b, zz)
            recv(("last", "C", k, "dn"), blk_c(zz, off(x, 1, NX)), x_dev(1))
            recv(("last", "C", k, "opp"), blk_c(zz, off(x, 2, NX)), x_dev(-1))
            core_send("C", k, buf_c, zz)

    def fill_head(lo, hi, source):
        for t in range(8):
            hi_t, y_t = divmod(t, NY)
            j = y_t * 2 + hi_t
            tile = source(t)
            head_a[lo:hi, j * WA:(j + 1) * WA] = tile[:, :WA]
            head_b[lo:hi, j * WB:(j + 1) * WB] = tile[:, WA:WA + WB]
            head_c[lo:hi, j * WB:(j + 1) * WB] = tile[:, WA + WB:]

    offset = (pop * 8 + tp) * VOC

    def compute_one(zz):
        def tokens(piece):
            return jnp.concatenate(
                [
                    jnp.concatenate([piece(cc, yy, hi * 2 + lo) for lo in range(2) for cc in range(2)], axis=0)
                    for yy in range(NY)
                    for hi in range(2)
                ],
                axis=1,
            )

        full = lax.dot_general(
            head_b[...], tokens(lambda cc, yy, xx: buf_b[zz, cc, yy, xx]), NT, preferred_element_type=F32
        )
        full += lax.dot_general(
            head_c[...], tokens(lambda cc, yy, xx: buf_c[zz, cc, xx, yy]), NT, preferred_element_type=F32
        )
        full += lax.dot_general(
            head_a[...], tokens(lambda cc, yy, xx: buf_a[zz, cc, yy, xx]), NT, preferred_element_type=F32
        )
        lane = lax.broadcasted_iota(jnp.int32, (FACT, 256), 1)
        column = lax.broadcasted_iota(jnp.int32, (FACT, 256), 0)
        lane_lo = lax.shift_right_logical(lane, 7)
        lane_c = lax.bitwise_and(lax.shift_right_logical(lane, 6), 1)
        pair = (lane_lo * NZ + zz) * 2 + lane_c
        odd = lax.bitwise_and(lax.shift_right_logical(lane, 5), 1)
        own = lax.shift_right_logical(column, 2) == pair
        sign = jnp.where(odd == 0, SIGMA_NOISE, -SIGMA_NOISE)
        lowrank = jnp.where(own, full[VOC:] * sign, 0.0).astype(BF16)
        logits = full[:VOC] + jnp.dot(left_ref[...], lowrank, preferred_element_type=F32)
        best = jnp.max(logits, axis=0, keepdims=True)
        total = jnp.sum(jnp.exp(logits - best), axis=0, keepdims=True)
        wanted = jnp.concatenate([tgt_ref[zz], tgt_ref[NZ + zz]], axis=1) - offset
        rows = lax.broadcasted_iota(jnp.int32, (VOC, 256), 0)
        target = jnp.sum(jnp.where(rows == wanted, logits, 0.0), axis=0, keepdims=True)
        packed = jnp.concatenate([best, total, target, jnp.zeros((5, 256), F32)], axis=0)
        st[zz, 0] = packed[:, :128]
        st[zz, 1] = packed[:, 128:]

    def compute(s):
        for k, way, _ in slots[s]:
            zz = slot_z(way, s, -1)
            for part, ref in (("A", buf_a), ("B", buf_b), ("C", buf_c)):
                recv(("core", part, k), ref.at[zz, sib], dev(x, y, z, sib))
        def body(i, carry):
            compute_one(off(z, -s + 2 * s * i, NZ))
            return carry

        lax.fori_loop(0, len(slots[s]), body, 0)

    for d in (1, 3, 2):
        src_x, src_y = plus(x, -d, NX), plus(y, -d, NY)
        recv(("B1", d), buf_b.at[z, c, y, src_x], dev(src_x, y, z, c))
        recv(("C1", d), buf_c.at[z, c, x, src_y], dev(x, src_y, z, c))
    z_start("B")
    z_start("C")
    last_send("B", 0, z)
    last_send("C", 0, z)
    for d in (1, 3, 2):
        src_x = plus(x, -d, NX)
        recv(("A1", d), buf_a.at[z, c, y, src_x], dev(src_x, y, z, c))
    for d in (1, 3, 2):
        send(("A2", d), buf_a.at[z, c, y], buf_a.at[z, c, y], dev(x, plus(y, d, NY), z, c))
    for d in range(1, 4):
        src_y = plus(y, -d, NY)
        recv(("Rt", d), rt.at[c, x_hi * NY + src_y], dev(x, src_y, z, c))
    send(("Rx",), rt.at[c, pl.ds(x_hi * NY, NY)], rt.at[c, pl.ds(x_hi * NY, NY)], mirror)

    load.wait()
    fill_head(0, VOC, lambda t: stage[:, t * FEAT:(t + 1) * FEAT].astype(BF16))

    for d in (1, 3, 2):
        src_y = plus(y, -d, NY)
        recv(("A2", d), buf_a.at[z, c, src_y], dev(x, src_y, z, c))
    z_start("A")

    z_recv(1)
    recv(("Rx",), rt.at[c, pl.ds((1 - x_hi) * NY, NY)], mirror)
    send(("Rd",), rt.at[c], rt.at[c], dev(x, y, z, sib))
    y_recv(0)
    z_recv(2)
    y_recv(1)
    o_recv(0)
    z_recv(3)
    y_recv(2)
    o_recv(1)
    recv(("Rd",), rt.at[sib], dev(x, y, z, sib))
    rt_copy = pltpu.make_async_copy(rt, rt_out_ref, lsem.at[1])
    rt_copy.start()
    fill_head(VOC, VOC + 64, lambda t: rt[0, t])
    fill_head(VOC + 64, AUG, lambda t: rt[1, t])
    compute(0)
    z_recv(4)
    y_recv(3)
    o_recv(2)
    compute(1)
    y_recv(4)
    o_recv(3)
    compute(2)
    compute(3)
    o_recv(4)
    compute(4)

    r1[pl.ds(blk, 1)] = st[z, x_lo][None]
    for d in range(1, 16):
        b = plus(blk, d, 16)
        send(("stat", 1, d), st.at[lax.rem(b, NZ), lax.div(b, NZ)], r1.at[blk], blk_dev(b))
    for d in range(1, 16):
        b = plus(blk, -d, 16)
        recv(("stat", 1, d), r1.at[b], blk_dev(b))
    best, total, target = combine(r1[...])
    packed = jnp.concatenate([best, total, target, jnp.zeros((5, 128), F32)], axis=0)
    r2[pl.ds(quad, 1)] = packed[None]
    for d in range(1, 16):
        send(("stat", 2, d), r2.at[quad], r2.at[quad], quad_dev(plus(quad, d, 16)))
    for d in range(1, 16):
        q = plus(quad, -d, 16)
        recv(("stat", 2, d), r2.at[q], quad_dev(q))
    best, total, target = combine(r2[...])
    logprob = target - best - jnp.log(total)
    lane = lax.broadcasted_iota(jnp.int32, (1, 128), 1)
    zero = jnp.zeros((1, 128), F32)
    means = [
        jnp.sum(jnp.where(lax.shift_right_logical(lane, 5) == m, logprob, 0.0), axis=1, keepdims=True) / 32.0
        for m in range(4)
    ]
    loglik, weights = zero, zero
    for m in range(4):
        loglik = jnp.where(lane == blk * 4 + m, means[m], loglik)
    for h in range(2):
        weights = jnp.where(lax.shift_right_logical(lane, 2) == blk * 2 + h, means[2 * h] - means[2 * h + 1], weights)
    packed = jnp.concatenate([loglik, weights, jnp.zeros((6, 128), F32)], axis=0)
    r3[pl.ds(blk, 1)] = packed[None]
    for d in range(1, 16):
        send(("stat", 3, d), r3.at[blk], r3.at[blk], blk_dev(plus(blk, d, 16)))
    for d in range(1, 16):
        b = plus(blk, -d, 16)
        recv(("stat", 3, d), r3.at[b], blk_dev(b))
    out_ref[...] = jnp.sum(r3[...], axis=0)
    for copy in sent:
        copy.wait_send()
    rt_copy.wait()


def update_kernel(w_ref, left_ref, rt_ref, master_ref, out_ref):
    scaled = (left_ref[...].astype(F32) * w_ref[1:2, :]).astype(BF16)
    right = jnp.concatenate([rt_ref[0, 0], rt_ref[1, 0]], axis=0)
    update = jnp.dot(scaled, right, preferred_element_type=F32)
    out_ref[...] = master_ref[...] + LEARN_RATE * update


def body(hidden, norm_gain, right_factors, left_factors, targets, master):
    vmem = pl.BlockSpec(memory_space=pltpu.VMEM)
    hbm = pl.BlockSpec(memory_space=pl.ANY)
    result, right_t = pl.pallas_call(
        gather_kernel,
        out_shape=(
            jax.ShapeDtypeStruct((8, 128), F32),
            jax.ShapeDtypeStruct((2, 8, 64, FEAT), BF16),
        ),
        in_specs=[vmem, vmem, vmem, vmem, vmem, hbm],
        out_specs=(vmem, hbm),
        scratch_shapes=[
            pltpu.VMEM((NZ, 2, NY, NX, ROWS, WA), BF16),
            pltpu.VMEM((NZ, 2, NY, NX, ROWS, WB), BF16),
            pltpu.VMEM((NZ, 2, NX, NY, ROWS, WB), BF16),
            pltpu.VMEM((AUG, 8 * WA), BF16),
            pltpu.VMEM((AUG, 8 * WB), BF16),
            pltpu.VMEM((AUG, 8 * WB), BF16),
            pltpu.VMEM((2, 8, 64, FEAT), BF16),
            pltpu.VMEM((VOC, D), F32),
            pltpu.VMEM((8, 8, 128), F32),
            pltpu.VMEM((NZ, 2, 8, 128), F32),
            pltpu.VMEM((16, 8, 128), F32),
            pltpu.VMEM((16, 8, 128), F32),
            pltpu.VMEM((16, 8, 128), F32),
            pltpu.SemaphoreType.DMA((N_MSG,)),
            pltpu.SemaphoreType.DMA((N_MSG,)),
            pltpu.SemaphoreType.DMA((2,)),
        ],
        compiler_params=pltpu.CompilerParams(
            collective_id=0, has_side_effects=True, vmem_limit_bytes=56 * 1024 * 1024
        ),
        name="gather_logits",
    )(
        hidden, norm_gain.reshape(1, FEAT), right_factors, left_factors,
        targets.reshape(16, 1, 128), master,
    )
    new_master = pl.pallas_call(
        update_kernel,
        out_shape=jax.ShapeDtypeStruct((VOC, D), F32),
        grid=(8,),
        in_specs=[
            pl.BlockSpec((8, 128), lambda i: (0, 0)),
            pl.BlockSpec((VOC, FACT), lambda i: (0, 0)),
            pl.BlockSpec((2, 1, 64, FEAT), lambda i: (0, i, 0, 0)),
            pl.BlockSpec((VOC, FEAT), lambda i: (0, i)),
        ],
        out_specs=pl.BlockSpec((VOC, FEAT), lambda i: (0, i)),
        name="update_master",
    )(result, left_factors, right_t, master)
    return (result[0, :64], new_master)


def solution(mesh):
    in_specs = (
        P("pop", "tp"),
        P("tp"),
        P("tp", None),
        P(("pop", "tp"), None),
        P(),
        P(("pop", "tp"), None),
    )
    out_specs = (P(), P(("pop", "tp"), None))
    return jax.shard_map(body, mesh=mesh, in_specs=in_specs, out_specs=out_specs, check_vma=False)
```

```python
import jax
import jax.numpy as jnp
from jax import lax
from jax.experimental import pallas as pl
from jax.experimental.pallas import tpu as pltpu
from jax.sharding import PartitionSpec as P

D = 5120
RANK = 4
NORM_EPS = 1e-06
SIGMA_NOISE = 0.25
LEARN_RATE = 0.5
NX, NY, NZ = 4, 4, 8
ROWS = 64
FEAT = 640
WA, WB = 128, 256
VOC = 304
FACT = 128
AUG = VOC + FACT
F32, BF16 = jnp.float32, jnp.bfloat16
MESH_ID = pl.DeviceIdType.MESH
NT = (((1,), (1,)), ((), ()))


class Ids:
    def __init__(self):
        self.table = {}

    def __call__(self, *key):
        return self.table.setdefault(key, len(self.table))


SLOTS = {0: [(0, "own", 0)], 4: [(7, "up", 4)]}
for _s in (1, 2, 3):
    SLOTS[_s] = [(2 * _s - 1, "up", _s), (2 * _s, "dn", _s)]
FINE = (5, 6, 7)


def message_names():
    ids = Ids()
    for dx in range(4):
        for dy in range(4):
            ids("sq", dx, dy)
    for d in range(1, 4):
        for kind in ("Rt", "B1", "C1", "A1", "A2"):
            ids(kind, d)
    ids("Rx")
    ids("Rd")
    for part in "ABC":
        for s in range(1, 5):
            ids("z", part, "up", s)
            if s < 4:
                ids("z", part, "dn", s)
    for k in range(8):
        for part in "BC":
            for way in ("up", "dn", "opp"):
                ids("last", part, k, way)
        for part in "ABC":
            if part != "A" and k in FINE:
                for piece in range(4):
                    ids("core", part, k, piece)
            else:
                ids("core", part, k)
    for i in range(2):
        for k in range(8):
            ids("stat1", i, k)
            ids("stat3", i, k)
            ids("stat2", i, k)
    return ids


IDS = message_names()
N_MSG = len(IDS.table)


def combine(stats):
    top = stats[:, 0, :]
    best = jnp.max(top, axis=0, keepdims=True)
    total = jnp.sum(stats[:, 1, :] * jnp.exp(top - best), axis=0, keepdims=True)
    target = jnp.sum(stats[:, 2, :], axis=0, keepdims=True)
    return best, total, target


def gather_kernel(
    hid_ref, gain_ref, right_ref, left_ref, tgt_ref, master_ref,
    out_ref, stage, rt,
    buf_a, buf_b, buf_c, head_a, head_b, head_c, raw_a, raw_b, raw_c, sq, st, r1, r2, r3,
    ssem, rsem, lsem,
):
    pop, tp = lax.axis_index("pop"), lax.axis_index("tp")
    c = lax.rem(pop, 2)
    z = lax.rem(lax.div(pop, 2), NZ)
    x_lo = lax.div(pop, 2 * NZ)
    x_hi = lax.div(tp, NY)
    y = lax.rem(tp, NY)
    x = x_hi * 2 + x_lo
    sib = 1 - c
    sgn = 1 - 2 * c
    blk = x_lo * NZ + z
    quad = c * 8 + tp

    xs = [lax.rem(x + k, NX) for k in range(NX)]
    ys = [lax.rem(y + k, NY) for k in range(NY)]
    zs = {k: lax.rem(z + k * sgn + NZ, NZ) for k in range(-4, 8)}
    xo = {k: lax.rem(x + k * sgn + NX, NX) for k in (-1, 0, 1, 2)}
    yo = {k: lax.rem(y + k * sgn + NY, NY) for k in (-1, 0, 1, 2)}
    los = (x_lo, 1 - x_lo)

    def dev(xx, yy, zz, cc):
        return ((lax.rem(xx, 2) * NZ + zz) * 2 + cc, lax.div(xx, 2) * NY + yy)

    sent = []

    def send(key, src, dst, device):
        i = IDS(*key)
        copy = pltpu.make_async_remote_copy(
            src_ref=src, dst_ref=dst, send_sem=ssem.at[i], recv_sem=rsem.at[i],
            device_id=device, device_id_type=MESH_ID,
        )
        copy.start()
        sent.append(copy)

    def recv(key, dst, device):
        i = IDS(*key)
        pltpu.make_async_remote_copy(
            src_ref=dst, dst_ref=dst, send_sem=ssem.at[i], recv_sem=rsem.at[i],
            device_id=device, device_id_type=MESH_ID,
        ).wait_recv()

    mirror = dev(3 - x, y, z, c)
    sibling = dev(x, y, z, sib)

    def plane(dx, dy):
        return dev(xs[dx], ys[dy], z, c)

    PLANE = [(dx, dy) for dx in range(NX) for dy in range(NY) if dx or dy]

    barrier = pltpu.get_barrier_semaphore()
    for dx, dy in PLANE:
        pl.semaphore_signal(barrier, inc=1, device_id=plane(dx, dy), device_id_type=MESH_ID)
    for device in (dev(x, y, zs[1], c), dev(x, y, zs[-1], c), sibling):
        pl.semaphore_signal(barrier, inc=1, device_id=device, device_id_type=MESH_ID)

    load = pltpu.make_async_copy(master_ref, stage, lsem.at[0])
    load.start()

    raw_a[pl.ds(x, 1)] = hid_ref[:, :WA][None]
    raw_b[pl.ds(x, 1)] = hid_ref[:, WA:WA + WB][None]
    raw_c[pl.ds(y, 1)] = hid_ref[:, WA + WB:][None]
    folded = jnp.zeros((ROWS, 128), F32)
    for j in range(FEAT // 128):
        piece = hid_ref[:, j * 128:(j + 1) * 128].astype(F32)
        folded = folded + piece * piece
    folded = jnp.concatenate([folded, jnp.zeros((128 - ROWS, 128), F32)], axis=0)
    row_sq = jnp.sum(folded.T, axis=0, keepdims=True)
    gains = [gain_ref[pl.ds(j * 128, 128)].reshape(1, 128) for j in range(FEAT // 128)]
    packed = jnp.concatenate([row_sq] + gains + [jnp.zeros((2, 128), F32)], axis=0)
    sq[pl.ds(x, 1), pl.ds(y, 1)] = packed[None, None]
    for j in range(FEAT // 128):
        block_t = right_ref[j * 128:(j + 1) * 128, :].astype(F32).T.astype(BF16)
        rt[c, pl.ds(tp, 1), :, j * 128:(j + 1) * 128] = jnp.where(c == 0, block_t[:64], block_t[64:])[None]

    pl.semaphore_wait(barrier, len(PLANE) + 3)

    for d in (1, 3, 2):
        send(("B1", d), raw_b.at[x], raw_b.at[x], plane(d, 0))
        send(("C1", d), raw_c.at[y], raw_c.at[y], plane(0, d))
    for dx, dy in PLANE:
        send(("sq", dx, dy), sq.at[x, y], sq.at[x, y], plane(dx, dy))
    for d in (1, 3, 2):
        send(("A1", d), raw_a.at[x], raw_a.at[x], plane(d, 0))
    for d in (1, 3, 2):
        send(("Rt", d), rt.at[c, tp], rt.at[c, tp], plane(0, d))

    def z_dev(k):
        return dev(x, y, zs[k], c)

    def y_dev(k):
        return dev(x, yo[k], z, c)

    def x_dev(k):
        return dev(xo[k], y, z, c)

    def blk_a(zz):
        return buf_a.at[zz, c]

    def blk_b(zz, yy):
        return buf_b.at[zz, c, yy]

    def blk_c(zz, xx):
        return buf_c.at[zz, c, xx]

    def z_blk(part, zz):
        return blk_a(zz) if part == "A" else blk_b(zz, y) if part == "B" else blk_c(zz, x)

    def slot_z(way, s, orient=1):
        return zs[-orient * s if way == "up" else orient * s]

    def last_send(part, k, zz):
        block = z_blk(part, zz)
        there = y_dev if part == "B" else x_dev
        send(("last", part, k, "up"), block, block, there(1))
        send(("last", part, k, "dn"), block, block, there(-1))
        if k in FINE:
            send(("core", part, k, 0), block, block, sibling)

    def z_start(part):
        send(("z", part, "up", 1), z_blk(part, z), z_blk(part, z), z_dev(1))
        send(("z", part, "dn", 1), z_blk(part, z), z_blk(part, z), z_dev(-1))

    def z_recv(s, parts):
        for part in parts:
            for k, way, _ in SLOTS[s]:
                zz = slot_z(way, s)
                step = 1 if way == "up" else -1
                recv(("z", part, way, s), z_blk(part, zz), z_dev(-step))
                if s < (4 if way == "up" else 3):
                    send(("z", part, way, s + 1), z_blk(part, zz), z_blk(part, zz), z_dev(step))
                if part == "A":
                    send(("core", "A", k), blk_a(zz), blk_a(zz), sibling)
                else:
                    last_send(part, k, zz)

    def last_blk(part, zz, k):
        return blk_b(zz, yo[k]) if part == "B" else blk_c(zz, xo[k])

    def y_recv(s):
        for k, way, _ in SLOTS[s]:
            zz = slot_z(way, s)
            for part, there in (("B", y_dev), ("C", x_dev)):
                below = last_blk(part, zz, -1)
                recv(("last", part, k, "up"), below, there(-1))
                send(("last", part, k, "opp"), below, below, there(1))
                if k in FINE:
                    send(("core", part, k, 1), below, below, sibling)

    def o_recv(s):
        for k, way, _ in SLOTS[s]:
            zz = slot_z(way, s)
            for part, ref, there in (("B", buf_b, y_dev), ("C", buf_c, x_dev)):
                above, opposite = last_blk(part, zz, 1), last_blk(part, zz, 2)
                recv(("last", part, k, "dn"), above, there(1))
                if k in FINE:
                    send(("core", part, k, 2), above, above, sibling)
                recv(("last", part, k, "opp"), opposite, there(-1))
                if k in FINE:
                    send(("core", part, k, 3), opposite, opposite, sibling)
                else:
                    send(("core", part, k), ref.at[zz, c], ref.at[zz, c], sibling)

    def core_recv(s):
        for k, way, _ in SLOTS[s]:
            zz = slot_z(way, s, -1)
            recv(("core", "A", k), buf_a.at[zz, sib], sibling)
            for part, ref, other in (("B", buf_b, yo), ("C", buf_c, xo)):
                if k in FINE:
                    for piece, at in ((0, 0), (1, 1), (2, -1), (3, 2)):
                        recv(("core", part, k, piece), ref.at[zz, sib, other[at]], sibling)
                else:
                    recv(("core", part, k), ref.at[zz, sib], sibling)

    def fill_head(lo, hi, source):
        for t in range(8):
            hi_t, y_t = divmod(t, NY)
            j = y_t * 2 + hi_t
            tile = source(t)
            head_a[lo:hi, j * WA:(j + 1) * WA] = tile[:, :WA]
            head_b[lo:hi, j * WB:(j + 1) * WB] = tile[:, WA:WA + WB]
            head_c[lo:hi, j * WB:(j + 1) * WB] = tile[:, WA + WB:]

    offset = (pop * 8 + tp) * VOC

    def compute_one(zz):
        def tokens(piece):
            return jnp.concatenate(
                [
                    jnp.concatenate([piece(cc, yy, hi * 2 + lo) for lo in range(2) for cc in range(2)], axis=0)
                    for yy in range(NY)
                    for hi in range(2)
                ],
                axis=1,
            )

        full = lax.dot_general(
            head_b[...], tokens(lambda cc, yy, xx: buf_b[zz, cc, yy, xx]), NT, preferred_element_type=F32
        )
        full += lax.dot_general(
            head_c[...], tokens(lambda cc, yy, xx: buf_c[zz, cc, xx, yy]), NT, preferred_element_type=F32
        )
        full += lax.dot_general(
            head_a[...], tokens(lambda cc, yy, xx: buf_a[zz, cc, yy, xx]), NT, preferred_element_type=F32
        )
        lane = lax.broadcasted_iota(jnp.int32, (FACT, 256), 1)
        column = lax.broadcasted_iota(jnp.int32, (FACT, 256), 0)
        lane_lo = lax.shift_right_logical(lane, 7)
        lane_c = lax.bitwise_and(lax.shift_right_logical(lane, 6), 1)
        pair = (lane_lo * NZ + zz) * 2 + lane_c
        odd = lax.bitwise_and(lax.shift_right_logical(lane, 5), 1)
        own = lax.shift_right_logical(column, 2) == pair
        sign = jnp.where(odd == 0, SIGMA_NOISE, -SIGMA_NOISE)
        lowrank = jnp.where(own, full[VOC:] * sign, 0.0).astype(BF16)
        logits = full[:VOC] + jnp.dot(left_ref[...], lowrank, preferred_element_type=F32)
        best = jnp.max(logits, axis=0, keepdims=True)
        total = jnp.sum(jnp.exp(logits - best), axis=0, keepdims=True)
        wanted = jnp.concatenate([tgt_ref[zz], tgt_ref[NZ + zz]], axis=1) - offset
        rows = lax.broadcasted_iota(jnp.int32, (VOC, 256), 0)
        target = jnp.sum(jnp.where(rows == wanted, logits, 0.0), axis=0, keepdims=True)
        packed = jnp.concatenate([best, total, target, jnp.zeros((5, 256), F32)], axis=0)
        st[zz, 0] = packed[:, :128]
        st[zz, 1] = packed[:, 128:]

    def stat_send(k):
        for i in range(2):
            if i or k:
                send(("stat1", i, k % 8), st.at[zs[k], los[i]], r1.at[blk], dev(x_hi * 2 + los[i], y, zs[k], c))

    def compute(s):
        core_recv(s)

        def loop(i, carry):
            compute_one(lax.rem(z + (2 * i - 1) * s + NZ, NZ))
            return carry

        if s in (0, 4):
            compute_one(zs[s])
        else:
            lax.fori_loop(0, 2, loop, 0)
        stat_send(s)
        if s in (1, 2, 3):
            stat_send(8 - s)

    for dx, dy in PLANE:
        recv(("sq", dx, dy), sq.at[xs[-dx], ys[-dy]], plane(-dx, -dy))
    scales = []
    for lo in range(2):
        total = sq[lo, :, 0, :] + sq[lo + 2, :, 0, :]
        row_scale = lax.rsqrt(jnp.sum(total, axis=0, keepdims=True) / D + NORM_EPS)
        scales.append(jnp.broadcast_to(row_scale, (128, 128)).T[:ROWS, :])
    own_scale = jnp.where(x_lo == 0, scales[0], scales[1])

    def normalize(values, scale, xx, yy, first, count):
        return jnp.concatenate(
            [
                (values[:, j * 128:(j + 1) * 128].astype(F32) * scale * sq[xx, yy, 1 + first + j:2 + first + j, :]).astype(BF16)
                for j in range(count)
            ],
            axis=1,
        )

    for d in (1, 3, 2):
        recv(("B1", d), raw_b.at[xs[-d]], plane(-d, 0))
    for t in range(NX):
        buf_b[z, c, y, t] = normalize(raw_b[t], scales[t % 2], t, y, 1, 2)
    z_start("B")
    last_send("B", 0, z)
    for d in (1, 3, 2):
        recv(("C1", d), raw_c.at[ys[-d]], plane(0, -d))
    for t in range(NY):
        buf_c[z, c, x, t] = normalize(raw_c[t], own_scale, x, t, 3, 2)
    z_start("C")
    last_send("C", 0, z)
    for d in (1, 3, 2):
        recv(("A1", d), raw_a.at[xs[-d]], plane(-d, 0))
    for t in range(NX):
        buf_a[z, c, y, t] = normalize(raw_a[t], scales[t % 2], t, y, 0, 1)
    for d in (1, 3, 2):
        send(("A2", d), buf_a.at[z, c, y], buf_a.at[z, c, y], plane(0, d))
    for d in range(1, 4):
        recv(("Rt", d), rt.at[c, x_hi * NY + ys[-d]], plane(0, -d))
    send(("Rx",), rt.at[c, pl.ds(x_hi * NY, NY)], rt.at[c, pl.ds(x_hi * NY, NY)], mirror)

    load.wait()
    fill_head(0, VOC, lambda t: stage[:, t * FEAT:(t + 1) * FEAT].astype(BF16))

    z_recv(1, "BC")
    y_recv(0)
    z_recv(2, "BC")
    for d in (1, 3, 2):
        recv(("A2", d), buf_a.at[z, c, ys[-d]], plane(0, -d))
    z_start("A")
    send(("core", "A", 0), blk_a(z), blk_a(z), sibling)
    recv(("Rx",), rt.at[c, pl.ds((1 - x_hi) * NY, NY)], mirror)
    send(("Rd",), rt.at[c], rt.at[c], sibling)
    y_recv(1)
    o_recv(0)
    z_recv(3, "BC")
    z_recv(1, "A")
    y_recv(2)
    o_recv(1)
    recv(("Rd",), rt.at[sib], sibling)
    fill_head(VOC, VOC + 64, lambda t: rt[0, t])
    fill_head(VOC + 64, AUG, lambda t: rt[1, t])
    compute(0)
    z_recv(4, "BC")
    z_recv(2, "A")
    compute(1)
    y_recv(3)
    o_recv(2)
    z_recv(3, "A")
    compute(2)
    y_recv(4)
    o_recv(3)
    z_recv(4, "A")
    o_recv(4)
    compute(3)
    compute(4)

    r1[pl.ds(blk, 1)] = st[z, x_lo][None]
    for copy in sent:
        copy.wait_send()
    sent.clear()
    for k in range(8):
        for i in range(2):
            if i or k:
                recv(("stat1", i, k), r1.at[los[i] * NZ + zs[-k if k < 5 else 8 - k]], dev(x_hi * 2 + los[i], y, zs[-k if k < 5 else 8 - k], c))
    best, total, target = combine(r1[...])
    packed = jnp.concatenate([best, total, target, jnp.zeros((5, 128), F32)], axis=0)
    r2[pl.ds(quad, 1)] = packed[None]

    def quad_at(i, k):
        h, d = divmod(k, 4)
        hi = x_hi if h == 0 else 1 - x_hi
        cc = c if i == 0 else sib
        return cc, hi, d

    QUAD = [(i, k) for i in range(2) for k in range(8) if i or k]
    for i, k in QUAD:
        cc, hi, d = quad_at(i, k)
        send(("stat2", i, k), r2.at[quad], r2.at[quad], dev(hi * 2 + x_lo, ys[d], z, cc))
    for i, k in QUAD:
        cc, hi, d = quad_at(i, k)
        recv(("stat2", i, k), r2.at[cc * 8 + hi * NY + ys[-d]], dev(hi * 2 + x_lo, ys[-d], z, cc))
    best, total, target = combine(r2[...])
    logprob = target - best - jnp.log(total)
    lane = lax.broadcasted_iota(jnp.int32, (1, 128), 1)
    zero = jnp.zeros((1, 128), F32)
    means = [
        jnp.sum(jnp.where(lax.shift_right_logical(lane, 5) == m, logprob, 0.0), axis=1, keepdims=True) / 32.0
        for m in range(4)
    ]
    loglik, weights = zero, zero
    for m in range(4):
        loglik = jnp.where(lane == blk * 4 + m, means[m], loglik)
    for h in range(2):
        weights = jnp.where(lax.shift_right_logical(lane, 2) == blk * 2 + h, means[2 * h] - means[2 * h + 1], weights)
    packed = jnp.concatenate([loglik, weights, jnp.zeros((6, 128), F32)], axis=0)
    r3[pl.ds(blk, 1)] = packed[None]
    for i, k in QUAD:
        send(("stat3", i, k), r3.at[blk], r3.at[blk], dev(x_hi * 2 + los[i], y, zs[k], c))
    for i, k in QUAD:
        zz = zs[-k if k < 5 else 8 - k]
        recv(("stat3", i, k), r3.at[los[i] * NZ + zz], dev(x_hi * 2 + los[i], y, zz, c))
    out_ref[...] = jnp.sum(r3[...], axis=0)
    for copy in sent:
        copy.wait_send()


def update_kernel(w_ref, left_ref, rt_ref, master_ref, ll_ref, out_ref, block, sems):
    ll_ref[...] = w_ref[0, :64]
    scaled = (left_ref[...].astype(F32) * w_ref[1:2, :]).astype(BF16)
    copies = []
    for t in range(8):
        cols = slice(t * FEAT, (t + 1) * FEAT)
        right = jnp.concatenate([rt_ref[0, t], rt_ref[1, t]], axis=0)
        update = jnp.dot(scaled, right, preferred_element_type=F32)
        block[:, cols] = master_ref[:, cols] + LEARN_RATE * update
        copy = pltpu.make_async_copy(block.at[:, cols], out_ref.at[:, cols], sems.at[t])
        copy.start()
        copies.append(copy)
    for copy in copies:
        copy.wait()


def body(hidden, norm_gain, right_factors, left_factors, targets, master):
    vmem = pl.BlockSpec(memory_space=pltpu.VMEM)
    hbm = pl.BlockSpec(memory_space=pl.ANY)
    result, stage, right_t = pl.pallas_call(
        gather_kernel,
        out_shape=(
            pltpu.VMEM((8, 128), F32),
            pltpu.VMEM((VOC, D), F32),
            pltpu.VMEM((2, 8, 64, FEAT), BF16),
        ),
        in_specs=[vmem, vmem, vmem, vmem, vmem, hbm],
        out_specs=(vmem, vmem, vmem),
        scratch_shapes=[
            pltpu.VMEM((NZ, 2, NY, NX, ROWS, WA), BF16),
            pltpu.VMEM((NZ, 2, NY, NX, ROWS, WB), BF16),
            pltpu.VMEM((NZ, 2, NX, NY, ROWS, WB), BF16),
            pltpu.VMEM((AUG, 8 * WA), BF16),
            pltpu.VMEM((AUG, 8 * WB), BF16),
            pltpu.VMEM((AUG, 8 * WB), BF16),
            pltpu.VMEM((NX, ROWS, WA), BF16),
            pltpu.VMEM((NX, ROWS, WB), BF16),
            pltpu.VMEM((NY, ROWS, WB), BF16),
            pltpu.VMEM((NX, NY, 8, 128), F32),
            pltpu.VMEM((NZ, 2, 8, 128), F32),
            pltpu.VMEM((16, 8, 128), F32),
            pltpu.VMEM((16, 8, 128), F32),
            pltpu.VMEM((16, 8, 128), F32),
            pltpu.SemaphoreType.DMA((N_MSG,)),
            pltpu.SemaphoreType.DMA((N_MSG,)),
            pltpu.SemaphoreType.DMA((1,)),
        ],
        compiler_params=pltpu.CompilerParams(
            collective_id=0, has_side_effects=True, vmem_limit_bytes=40 * 1024 * 1024
        ),
        name="gather_logits",
    )(
        hidden, norm_gain, right_factors, left_factors,
        targets.reshape(16, 1, 128), master,
    )
    loglik, new_master = pl.pallas_call(
        update_kernel,
        out_shape=(jax.ShapeDtypeStruct((64,), F32), jax.ShapeDtypeStruct((VOC, D), F32)),
        in_specs=[vmem, vmem, vmem, vmem],
        out_specs=(vmem, hbm),
        scratch_shapes=[pltpu.VMEM((VOC, D), F32), pltpu.SemaphoreType.DMA((8,))],
        compiler_params=pltpu.CompilerParams(vmem_limit_bytes=20 * 1024 * 1024),
        name="update_master",
    )(result, left_factors, right_t, stage)
    return (loglik, new_master)


def solution(mesh):
    in_specs = (
        P("pop", "tp"),
        P("tp"),
        P("tp", None),
        P(("pop", "tp"), None),
        P(),
        P(("pop", "tp"), None),
    )
    out_specs = (P(), P(("pop", "tp"), None))
    return jax.shard_map(body, mesh=mesh, in_specs=in_specs, out_specs=out_specs, check_vma=False)
```

```python
import jax
import jax.numpy as jnp
from jax import lax
from jax.experimental import pallas as pl
from jax.experimental.pallas import tpu as pltpu
from jax.sharding import PartitionSpec as P

D = 5120
RANK = 4
NORM_EPS = 1e-06
SIGMA_NOISE = 0.25
LEARN_RATE = 0.5
NX, NY, NZ = 4, 4, 8
ROWS = 64
FEAT = 640
WA, WB = 128, 256
VOC = 304
FACT = 128
AUG = VOC + FACT
F32, BF16 = jnp.float32, jnp.bfloat16
MESH_ID = pl.DeviceIdType.MESH
NT = (((1,), (1,)), ((), ()))


class Ids:
    def __init__(self):
        self.table = {}

    def __call__(self, *key):
        return self.table.setdefault(key, len(self.table))


SLOTS = {0: ("own", 0), 7: ("up", 4)}
for _s in (1, 2, 3):
    SLOTS[2 * _s - 1], SLOTS[2 * _s] = ("up", _s), ("dn", _s)
SLOT_OF = {where: k for k, where in SLOTS.items()}
SND = "snd"
RING = "z"
LAST = "y"
A = "A"
B = "B"
C = "C"
UP = "up"
DN = "dn"
OPP = "opp"
COMP = "comp"
RIGHT_Y = "Rtr"
RIGHT_X = "Rxr"
RIGHT_CORE = "Rdr"
HEAD = "head"
A_PLANE = "A2r"
FINE = (3, 4, 5, 6, 7)
ORDER = (
    (SND, LAST, B, 0, UP), (SND, LAST, B, 0, DN), (SND, RING, B, UP, 1),
    (SND, RING, B, DN, 1), (SND, LAST, C, 0, UP), (SND, LAST, C, 0, DN),
    (SND, RING, C, UP, 1), (SND, RING, C, DN, 1), (RIGHT_Y,), (HEAD,), (RING, B, UP, 1),
    (SND, LAST, B, 1, UP), (SND, LAST, B, 1, DN), (SND, RING, B, UP, 2), (LAST, B, 0, UP),
    (SND, LAST, B, 0, OPP), (LAST, C, 0, UP), (SND, LAST, C, 0, OPP), (LAST, B, 0, DN),
    (RING, B, DN, 1), (SND, RING, B, DN, 2), (SND, LAST, B, 2, UP), (SND, LAST, B, 2, DN),
    (LAST, C, 0, DN), (RING, C, UP, 1), (SND, LAST, C, 1, UP), (SND, LAST, C, 1, DN),
    (SND, RING, C, UP, 2), (RING, C, DN, 1), (SND, RING, C, DN, 2), (SND, LAST, C, 2, UP),
    (SND, LAST, C, 2, DN), (LAST, B, 1, UP), (SND, LAST, B, 1, OPP), (RING, B, UP, 2),
    (SND, RING, B, UP, 3), (SND, LAST, B, 3, UP), (SND, LAST, B, 3, DN), (A_PLANE,),
    (SND, RING, A, UP, 1), (SND, RING, A, DN, 1), (RING, B, DN, 2), (SND, RING, B, DN, 3),
    (SND, LAST, B, 4, UP), (SND, LAST, B, 4, DN), (LAST, B, 1, DN), (LAST, B, 0, OPP),
    (RING, C, UP, 2), (SND, RING, C, UP, 3), (SND, LAST, C, 3, UP), (SND, LAST, C, 3, DN),
    (RIGHT_X,), (LAST, B, 2, UP), (SND, LAST, B, 2, OPP), (RING, C, DN, 2), (SND, RING, C, DN, 3),
    (SND, LAST, C, 4, UP), (SND, LAST, C, 4, DN), (LAST, C, 0, OPP), (LAST, B, 2, DN),
    (RING, B, UP, 3), (SND, RING, B, UP, 4), (SND, LAST, B, 5, UP), (SND, LAST, B, 5, DN),
    (LAST, C, 1, UP), (SND, LAST, C, 1, OPP), (LAST, B, 1, OPP), (RIGHT_CORE,), (LAST, B, 3, UP),
    (SND, LAST, B, 3, OPP), (RING, A, UP, 1), (SND, RING, A, UP, 2), (LAST, C, 1, DN),
    (COMP, 0), (LAST, C, 2, UP), (SND, LAST, C, 2, OPP), (LAST, C, 2, DN), (LAST, B, 3, DN),
    (LAST, B, 4, UP), (SND, LAST, B, 4, OPP), (RING, A, DN, 1), (SND, RING, A, DN, 2),
    (LAST, C, 3, UP), (SND, LAST, C, 3, OPP), (LAST, B, 4, DN), (RING, B, DN, 3),
    (SND, LAST, B, 6, UP), (SND, LAST, B, 6, DN), (LAST, C, 3, DN), (LAST, B, 2, OPP),
    (RING, C, UP, 3), (SND, RING, C, UP, 4), (SND, LAST, C, 5, UP), (SND, LAST, C, 5, DN),
    (LAST, C, 4, UP), (SND, LAST, C, 4, OPP), (LAST, B, 5, UP), (SND, LAST, B, 5, OPP),
    (RING, C, DN, 3), (SND, LAST, C, 6, UP), (SND, LAST, C, 6, DN), (LAST, C, 4, DN),
    (LAST, B, 5, DN), (RING, B, UP, 4), (SND, LAST, B, 7, UP), (SND, LAST, B, 7, DN),
    (LAST, C, 1, OPP), (LAST, B, 3, OPP), (LAST, C, 2, OPP), (LAST, B, 4, OPP), (RING, A, UP, 2),
    (SND, RING, A, UP, 3), (COMP, 1), (LAST, B, 6, UP), (SND, LAST, B, 6, OPP),
    (LAST, C, 5, UP), (SND, LAST, C, 5, OPP), (LAST, C, 3, OPP), (LAST, B, 6, DN),
    (RING, A, DN, 2), (SND, RING, A, DN, 3), (COMP, 2), (RING, C, UP, 4),
    (SND, LAST, C, 7, UP), (SND, LAST, C, 7, DN), (LAST, C, 4, OPP), (LAST, B, 5, OPP),
    (LAST, B, 7, UP), (SND, LAST, B, 7, OPP), (LAST, C, 5, DN), (COMP, 3), (RING, A, UP, 3),
    (SND, RING, A, UP, 4), (LAST, C, 6, UP), (SND, LAST, C, 6, OPP), (LAST, B, 6, OPP),
    (LAST, C, 6, DN), (LAST, B, 7, DN), (COMP, 4), (RING, A, DN, 3), (LAST, C, 7, UP),
    (SND, LAST, C, 7, OPP), (LAST, C, 5, OPP), (LAST, B, 7, OPP), (LAST, C, 7, DN),
    (LAST, C, 6, OPP), (RING, A, UP, 4), (COMP, 5), (LAST, C, 7, OPP), (COMP, 6), (COMP, 7),
)


def message_names():
    ids = Ids()
    for dx in range(4):
        for dy in range(4):
            ids("sq", dx, dy)
    for d in range(1, 4):
        for kind in ("Rt", "B1", "C1", "A1", "A2"):
            ids(kind, d)
    ids("Rx")
    ids("Rd")
    for part in "ABC":
        for s in range(1, 5):
            ids("z", part, "up", s)
            if s < 4:
                ids("z", part, "dn", s)
    for k in range(8):
        for part in "BC":
            for way in ("up", "dn", "opp"):
                ids("last", part, k, way)
        for part in "ABC":
            if part != "A" and k in FINE:
                for piece in range(4):
                    ids("core", part, k, piece)
            else:
                ids("core", part, k)
    for i in range(2):
        for k in range(8):
            ids("stat1", i, k)
            ids("stat3", i, k)
            ids("stat2", i, k)
    return ids


IDS = message_names()
N_MSG = len(IDS.table)


def combine(stats):
    top = stats[:, 0, :]
    best = jnp.max(top, axis=0, keepdims=True)
    total = jnp.sum(stats[:, 1, :] * jnp.exp(top - best), axis=0, keepdims=True)
    target = jnp.sum(stats[:, 2, :], axis=0, keepdims=True)
    return best, total, target


def gather_kernel(
    hid_in, gain_in, right_in, left_in, tgt_in, master_ref,
    out_ref, stage, rt,
    hid_ref, gain_ref, right_ref, left_ref, tgt_ref, buf_a, buf_b, buf_c, head, acc, raw_a, raw_b, raw_c, sq, st, r1, r2, r3,
    ssem, rsem, lsem,
):
    pop, tp = lax.axis_index("pop"), lax.axis_index("tp")
    c = lax.rem(pop, 2)
    z = lax.rem(lax.div(pop, 2), NZ)
    x_lo = lax.div(pop, 2 * NZ)
    x_hi = lax.div(tp, NY)
    y = lax.rem(tp, NY)
    x = x_hi * 2 + x_lo
    sib = 1 - c
    sgn = 1 - 2 * c
    blk = x_lo * NZ + z
    quad = c * 8 + tp

    xs = [lax.rem(x + k, NX) for k in range(NX)]
    ys = [lax.rem(y + k, NY) for k in range(NY)]
    zs = {k: lax.rem(z + k * sgn + NZ, NZ) for k in range(-4, 8)}
    xo = {k: lax.rem(x + k * sgn + NX, NX) for k in (-1, 0, 1, 2)}
    yo = {k: lax.rem(y + k * sgn + NY, NY) for k in (-1, 0, 1, 2)}
    los = (x_lo, 1 - x_lo)

    def dev(xx, yy, zz, cc):
        return ((lax.rem(xx, 2) * NZ + zz) * 2 + cc, lax.div(xx, 2) * NY + yy)

    sent = []

    def send(key, src, dst, device):
        i = IDS(*key)
        copy = pltpu.make_async_remote_copy(
            src_ref=src, dst_ref=dst, send_sem=ssem.at[i], recv_sem=rsem.at[i],
            device_id=device, device_id_type=MESH_ID,
        )
        copy.start()
        sent.append(copy)

    def recv(key, dst, device):
        i = IDS(*key)
        pltpu.make_async_remote_copy(
            src_ref=dst, dst_ref=dst, send_sem=ssem.at[i], recv_sem=rsem.at[i],
            device_id=device, device_id_type=MESH_ID,
        ).wait_recv()

    mirror = dev(3 - x, y, z, c)
    sibling = dev(x, y, z, sib)

    def plane(dx, dy):
        return dev(xs[dx], ys[dy], z, c)

    far = (2, 1, 3, 0)
    PLANE = [(dx, dy) for dx in far for dy in far if dx or dy]

    barrier = pltpu.get_barrier_semaphore()
    for dx, dy in PLANE:
        pl.semaphore_signal(barrier, inc=1, device_id=plane(dx, dy), device_id_type=MESH_ID)
    for device in (dev(x, y, zs[1], c), dev(x, y, zs[-1], c), sibling):
        pl.semaphore_signal(barrier, inc=1, device_id=device, device_id_type=MESH_ID)

    loads = [
        pltpu.make_async_copy(src, dst, lsem.at[i])
        for i, (src, dst) in enumerate(
            (
                (hid_in, hid_ref), (gain_in, gain_ref), (right_in, right_ref),
                (left_in, left_ref), (tgt_in, tgt_ref), (master_ref, stage),
            )
        )
    ]
    for load in loads:
        load.start()
    loads[0].wait()

    raw_a[pl.ds(x, 1)] = hid_ref[:, :WA][None]
    raw_b[pl.ds(x, 1)] = hid_ref[:, WA:WA + WB][None]
    raw_c[pl.ds(y, 1)] = hid_ref[:, WA + WB:][None]
    folded = jnp.zeros((ROWS, 128), F32)
    for j in range(FEAT // 128):
        piece = hid_ref[:, j * 128:(j + 1) * 128].astype(F32)
        folded = folded + piece * piece
    folded = jnp.concatenate([folded, jnp.zeros((128 - ROWS, 128), F32)], axis=0)
    row_sq = jnp.sum(folded.T, axis=0, keepdims=True)
    loads[1].wait()
    gains = [gain_ref[pl.ds(j * 128, 128)].reshape(1, 128) for j in range(FEAT // 128)]
    packed = jnp.concatenate([row_sq] + gains + [jnp.zeros((2, 128), F32)], axis=0)
    sq[pl.ds(x, 1), pl.ds(y, 1)] = packed[None, None]
    pl.semaphore_wait(barrier, len(PLANE) + 3)

    for dx, dy in PLANE:
        send(("sq", dx, dy), sq.at[x, y], sq.at[x, y], plane(dx, dy))
    for d in (2, 1, 3):
        send(("B1", d), raw_b.at[x], raw_b.at[x], plane(d, 0))
        send(("C1", d), raw_c.at[y], raw_c.at[y], plane(0, d))
    for d in (1, 3, 2):
        send(("A1", d), raw_a.at[x], raw_a.at[x], plane(d, 0))
    loads[2].wait()
    for j in range(FEAT // 128):
        block_t = right_ref[j * 128:(j + 1) * 128, :].astype(F32).T.astype(BF16)
        rt[c, pl.ds(tp, 1), :, j * 128:(j + 1) * 128] = jnp.where(c == 0, block_t[:64], block_t[64:])[None]
    for d in (1, 3, 2):
        send(("Rt", d), rt.at[c, tp], rt.at[c, tp], plane(0, d))

    def z_dev(k):
        return dev(x, y, zs[k], c)

    def y_dev(k):
        return dev(x, yo[k], z, c)

    def x_dev(k):
        return dev(xo[k], y, z, c)

    def blk_a(zz):
        return buf_a.at[zz, c]

    def blk_b(zz, yy):
        return buf_b.at[zz, c, yy]

    def blk_c(zz, xx):
        return buf_c.at[zz, c, xx]

    def z_blk(part, zz):
        return blk_a(zz) if part == "A" else blk_b(zz, y) if part == "B" else blk_c(zz, x)

    def slot_z(way, s, orient=1):
        return zs[-orient * s if way == "up" else orient * s]

    def hand_over(part, k, zz):
        if k in FINE:
            send(("core", part, k, 0), z_blk(part, zz), z_blk(part, zz), sibling)

    def last_blk(part, zz, k):
        return blk_b(zz, yo[k]) if part == "B" else blk_c(zz, xo[k])

    def ring_send(part, way, s):
        block = z_blk(part, slot_z(way, s - 1))
        send(("z", part, way, s), block, block, z_dev(1 if way == "up" else -1))

    def last_send(part, k, way):
        zz = slot_z(*SLOTS[k])
        block = last_blk(part, zz, -1 if way == "opp" else 0)
        there = y_dev if part == "B" else x_dev
        send(("last", part, k, way), block, block, there(-1 if way == "dn" else 1))

    def take_z(part, way, s):
        k = SLOT_OF[way, s]
        zz = slot_z(way, s)
        block = z_blk(part, zz)
        recv(("z", part, way, s), block, z_dev(-1 if way == "up" else 1))
        if part == "A":
            send(("core", "A", k), block, block, sibling)
        else:
            hand_over(part, k, zz)

    pieces_in = {}

    def take_last(part, k, way):
        zz = slot_z(*SLOTS[k])
        there = y_dev if part == "B" else x_dev
        block = last_blk(part, zz, {"up": -1, "dn": 1, "opp": 2}[way])
        recv(("last", part, k, way), block, there(1 if way == "dn" else -1))
        if k in FINE:
            send(("core", part, k, {"up": 1, "dn": 2, "opp": 3}[way]), block, block, sibling)
        else:
            pieces_in[part, k] = pieces_in.get((part, k), 0) + 1
            if pieces_in[part, k] == 3:
                whole = (buf_b if part == "B" else buf_c).at[zz, c]
                send(("core", part, k), whole, whole, sibling)

    def core_recv(k, zz):
        recv(("core", "A", k), buf_a.at[zz, sib], sibling)
        for part, ref, other in (("B", buf_b, yo), ("C", buf_c, xo)):
            if k in FINE:
                for piece, at in ((0, 0), (1, 1), (2, -1), (3, 2)):
                    recv(("core", part, k, piece), ref.at[zz, sib, other[at]], sibling)
            else:
                recv(("core", part, k), ref.at[zz, sib], sibling)

    def fill_head(lo, hi, source):
        for t in range(8):
            hi_t, y_t = divmod(t, NY)
            tile = source(t)
            head[y_t, lo:hi, hi_t * WA:(hi_t + 1) * WA] = tile[:, :WA]
            head[y_t, lo:hi, 2 * WA + hi_t * WB:2 * WA + (hi_t + 1) * WB] = tile[:, WA:WA + WB]
            head[y_t, lo:hi, 2 * (WA + WB) + hi_t * WB:2 * (WA + WB) + (hi_t + 1) * WB] = tile[:, WA + WB:]

    offset = (pop * 8 + tp) * VOC

    def compute_one(zz):
        def tokens(piece, hi):
            return jnp.concatenate([piece(cc, hi * 2 + lo) for lo in range(2) for cc in range(2)], axis=0)

        def features(yy, carry):
            columns = [tokens(lambda cc, xx: buf_a[zz, cc, yy, xx], hi) for hi in range(2)]
            columns += [tokens(lambda cc, xx: buf_b[zz, cc, yy, xx], hi) for hi in range(2)]
            columns += [tokens(lambda cc, xx: buf_c[zz, cc, xx, yy], hi) for hi in range(2)]
            acc[...] += lax.dot_general(
                head[yy], jnp.concatenate(columns, axis=1), NT, preferred_element_type=F32
            )
            return carry

        acc[...] = jnp.zeros((AUG, 256), F32)
        lax.fori_loop(0, NY, features, 0)
        full = acc[...]
        lane = lax.broadcasted_iota(jnp.int32, (FACT, 256), 1)
        column = lax.broadcasted_iota(jnp.int32, (FACT, 256), 0)
        lane_lo = lax.shift_right_logical(lane, 7)
        lane_c = lax.bitwise_and(lax.shift_right_logical(lane, 6), 1)
        pair = (lane_lo * NZ + zz) * 2 + lane_c
        odd = lax.bitwise_and(lax.shift_right_logical(lane, 5), 1)
        own = lax.shift_right_logical(column, 2) == pair
        sign = jnp.where(odd == 0, SIGMA_NOISE, -SIGMA_NOISE)
        lowrank = jnp.where(own, full[VOC:] * sign, 0.0).astype(BF16)
        logits = full[:VOC] + jnp.dot(left_ref[...], lowrank, preferred_element_type=F32)
        best = jnp.max(logits, axis=0, keepdims=True)
        total = jnp.sum(jnp.exp(logits - best), axis=0, keepdims=True)
        wanted = jnp.concatenate([tgt_ref[zz], tgt_ref[NZ + zz]], axis=1) - offset
        rows = lax.broadcasted_iota(jnp.int32, (VOC, 256), 0)
        target = jnp.sum(jnp.where(rows == wanted, logits, 0.0), axis=0, keepdims=True)
        packed = jnp.concatenate([best, total, target, jnp.zeros((5, 256), F32)], axis=0)
        st[zz, 0] = packed[:, :128]
        st[zz, 1] = packed[:, 128:]

    def stat_send(k):
        for i in range(2):
            if i or k:
                send(("stat1", i, k), st.at[zs[(k + 4) % 8], los[i]], r1.at[blk], dev(x_hi * 2 + los[i], y, zs[k], c))

    def compute(k):
        way, s = SLOTS[k]
        zz = slot_z(way, s, -1)
        core_recv(k, zz)
        compute_one(zz)
        stat_send(((8 - s if way == "dn" else s) + 4) % 8)

    def step(what, *which):
        if what == "snd":
            (ring_send if which[0] == "z" else last_send)(*which[1:])
        elif what == "z":
            take_z(*which)
        elif what == "y":
            take_last(*which)
        elif what == "comp":
            compute(*which)
        elif what == "head":
            for load in loads[3:]:
                load.wait()
            fill_head(0, VOC, lambda t: stage[:, t * FEAT:(t + 1) * FEAT].astype(BF16))
        elif what == "A2r":
            for d in (1, 3, 2):
                recv(("A2", d), buf_a.at[z, c, ys[-d]], plane(0, -d))
            send(("core", "A", 0), blk_a(z), blk_a(z), sibling)
        elif what == "Rtr":
            for d in range(1, 4):
                recv(("Rt", d), rt.at[c, x_hi * NY + ys[-d]], plane(0, -d))
            send(("Rx",), rt.at[c, pl.ds(x_hi * NY, NY)], rt.at[c, pl.ds(x_hi * NY, NY)], mirror)
        elif what == "Rxr":
            recv(("Rx",), rt.at[c, pl.ds((1 - x_hi) * NY, NY)], mirror)
            send(("Rd",), rt.at[c], rt.at[c], sibling)
        else:
            recv(("Rd",), rt.at[sib], sibling)
            fill_head(VOC, VOC + 64, lambda t: rt[0, t])
            fill_head(VOC + 64, AUG, lambda t: rt[1, t])

    def follow(first, part):
        at = first
        while at < len(ORDER):
            action = ORDER[at]
            if part is not None and not (action[0] == "snd" and action[2] == part):
                break
            step(*action)
            at += 1
        return at

    for dx, dy in PLANE:
        recv(("sq", dx, dy), sq.at[xs[-dx], ys[-dy]], plane(-dx, -dy))
    scales = []
    for lo in range(2):
        total = sq[lo, :, 0, :] + sq[lo + 2, :, 0, :]
        row_scale = lax.rsqrt(jnp.sum(total, axis=0, keepdims=True) / D + NORM_EPS)
        scales.append(jnp.broadcast_to(row_scale, (128, 128)).T[:ROWS, :])
    own_scale = jnp.where(x_lo == 0, scales[0], scales[1])

    def normalize(values, scale, xx, yy, first, count):
        return jnp.concatenate(
            [
                (values[:, j * 128:(j + 1) * 128].astype(F32) * scale * sq[xx, yy, 1 + first + j:2 + first + j, :]).astype(BF16)
                for j in range(count)
            ],
            axis=1,
        )

    for d in (1, 3, 2):
        recv(("B1", d), raw_b.at[xs[-d]], plane(-d, 0))
    for t in range(NX):
        buf_b[z, c, y, t] = normalize(raw_b[t], scales[t % 2], t, y, 1, 2)
    hand_over("B", 0, z)
    start_from = follow(0, "B")
    for d in (1, 3, 2):
        recv(("C1", d), raw_c.at[ys[-d]], plane(0, -d))
    for t in range(NY):
        buf_c[z, c, x, t] = normalize(raw_c[t], own_scale, x, t, 3, 2)
    hand_over("C", 0, z)
    start_from = follow(start_from, "C")
    for d in (1, 3, 2):
        recv(("A1", d), raw_a.at[xs[-d]], plane(-d, 0))
    for t in range(NX):
        buf_a[z, c, y, t] = normalize(raw_a[t], scales[t % 2], t, y, 0, 1)
    for d in (1, 3, 2):
        send(("A2", d), buf_a.at[z, c, y], buf_a.at[z, c, y], plane(0, d))

    follow(start_from, None)

    r1[pl.ds(blk, 1)] = st[zs[4], x_lo][None]
    for copy in sent:
        copy.wait_send()
    sent.clear()
    for k in range(8):
        for i in range(2):
            if i or k:
                recv(("stat1", i, k), r1.at[los[i] * NZ + zs[-k if k < 5 else 8 - k]], dev(x_hi * 2 + los[i], y, zs[-k if k < 5 else 8 - k], c))
    best, total, target = combine(r1[...])
    packed = jnp.concatenate([best, total, target, jnp.zeros((5, 128), F32)], axis=0)
    r2[pl.ds(quad, 1)] = packed[None]

    def quad_at(i, k):
        h, d = divmod(k, 4)
        hi = x_hi if h == 0 else 1 - x_hi
        cc = c if i == 0 else sib
        return cc, hi, d

    QUAD = [(i, k) for i in (1, 0) for k in (6, 2, 5, 7, 1, 3, 4, 0) if i or k]
    RING = [(i, k) for i in (1, 0) for k in (4, 3, 5, 2, 6, 1, 7, 0) if i or k]
    for i, k in QUAD:
        cc, hi, d = quad_at(i, k)
        send(("stat2", i, k), r2.at[quad], r2.at[quad], dev(hi * 2 + x_lo, ys[d], z, cc))
    for i, k in QUAD:
        cc, hi, d = quad_at(i, k)
        recv(("stat2", i, k), r2.at[cc * 8 + hi * NY + ys[-d]], dev(hi * 2 + x_lo, ys[-d], z, cc))
    best, total, target = combine(r2[...])
    logprob = target - best - jnp.log(total)
    lane = lax.broadcasted_iota(jnp.int32, (1, 128), 1)
    zero = jnp.zeros((1, 128), F32)
    means = [
        jnp.sum(jnp.where(lax.shift_right_logical(lane, 5) == m, logprob, 0.0), axis=1, keepdims=True) / 32.0
        for m in range(4)
    ]
    loglik, weights = zero, zero
    owned = x_lo * NZ + zs[4]
    for m in range(4):
        loglik = jnp.where(lane == owned * 4 + m, means[m], loglik)
    for h in range(2):
        weights = jnp.where(lax.shift_right_logical(lane, 2) == owned * 2 + h, means[2 * h] - means[2 * h + 1], weights)
    packed = jnp.concatenate([loglik, weights, jnp.zeros((6, 128), F32)], axis=0)
    r3[pl.ds(blk, 1)] = packed[None]
    for i, k in RING:
        send(("stat3", i, k), r3.at[blk], r3.at[blk], dev(x_hi * 2 + los[i], y, zs[k], c))
    for i, k in RING:
        zz = zs[-k if k < 5 else 8 - k]
        recv(("stat3", i, k), r3.at[los[i] * NZ + zz], dev(x_hi * 2 + los[i], y, zz, c))
    out_ref[...] = jnp.sum(r3[...], axis=0)
    for copy in sent:
        copy.wait_send()


def update_kernel(w_ref, left_ref, rt_ref, master_ref, ll_ref, out_ref, block, sems):
    ll_ref[...] = w_ref[0, :64]
    scaled = (left_ref[...].astype(F32) * w_ref[1:2, :]).astype(BF16)
    copies = []
    for t in range(8):
        cols = slice(t * FEAT, (t + 1) * FEAT)
        right = jnp.concatenate([rt_ref[0, t], rt_ref[1, t]], axis=0)
        update = jnp.dot(scaled, right, preferred_element_type=F32)
        block[:, cols] = master_ref[:, cols] + LEARN_RATE * update
        copy = pltpu.make_async_copy(block.at[:, cols], out_ref.at[:, cols], sems.at[t])
        copy.start()
        copies.append(copy)
    for copy in copies:
        copy.wait()


def body(hidden, norm_gain, right_factors, left_factors, targets, master):
    vmem = pl.BlockSpec(memory_space=pltpu.VMEM)
    hbm = pl.BlockSpec(memory_space=pl.ANY)
    result, stage, right_t = pl.pallas_call(
        gather_kernel,
        out_shape=(
            pltpu.VMEM((8, 128), F32),
            pltpu.VMEM((VOC, D), F32),
            pltpu.VMEM((2, 8, 64, FEAT), BF16),
        ),
        in_specs=[hbm] * 6,
        out_specs=(vmem, vmem, vmem),
        scratch_shapes=[
            pltpu.VMEM((ROWS, FEAT), BF16),
            pltpu.VMEM((FEAT,), F32),
            pltpu.VMEM((FEAT, FACT), BF16),
            pltpu.VMEM((VOC, FACT), BF16),
            pltpu.VMEM((16, 1, 128), jnp.int32),
            pltpu.VMEM((NZ, 2, NY, NX, ROWS, WA), BF16),
            pltpu.VMEM((NZ, 2, NY, NX, ROWS, WB), BF16),
            pltpu.VMEM((NZ, 2, NX, NY, ROWS, WB), BF16),
            pltpu.VMEM((NY, AUG, 2 * FEAT), BF16),
            pltpu.VMEM((AUG, 256), F32),
            pltpu.VMEM((NX, ROWS, WA), BF16),
            pltpu.VMEM((NX, ROWS, WB), BF16),
            pltpu.VMEM((NY, ROWS, WB), BF16),
            pltpu.VMEM((NX, NY, 8, 128), F32),
            pltpu.VMEM((NZ, 2, 8, 128), F32),
            pltpu.VMEM((16, 8, 128), F32),
            pltpu.VMEM((16, 8, 128), F32),
            pltpu.VMEM((16, 8, 128), F32),
            pltpu.SemaphoreType.DMA((N_MSG,)),
            pltpu.SemaphoreType.DMA((N_MSG,)),
            pltpu.SemaphoreType.DMA((6,)),
        ],
        compiler_params=pltpu.CompilerParams(
            collective_id=0, has_side_effects=True, vmem_limit_bytes=52 * 1024 * 1024
        ),
        name="gather_logits",
    )(
        hidden, norm_gain, right_factors, left_factors,
        targets.reshape(16, 1, 128), master,
    )
    loglik, new_master = pl.pallas_call(
        update_kernel,
        out_shape=(jax.ShapeDtypeStruct((64,), F32), jax.ShapeDtypeStruct((VOC, D), F32)),
        in_specs=[vmem, vmem, vmem, vmem],
        out_specs=(vmem, hbm),
        scratch_shapes=[pltpu.VMEM((VOC, D), F32), pltpu.SemaphoreType.DMA((8,))],
        compiler_params=pltpu.CompilerParams(vmem_limit_bytes=20 * 1024 * 1024),
        name="update_master",
    )(result, left_factors, right_t, stage)
    return (loglik, new_master)


def solution(mesh):
    in_specs = (
        P("pop", "tp"),
        P("tp"),
        P("tp", None),
        P(("pop", "tp"), None),
        P(),
        P(("pop", "tp"), None),
    )
    out_specs = (P(), P(("pop", "tp"), None))
    return jax.shard_map(body, mesh=mesh, in_specs=in_specs, out_specs=out_specs, check_vma=False)
```

```python
import jax
import jax.numpy as jnp
from jax import lax
from jax.experimental import pallas as pl
from jax.experimental.pallas import tpu as pltpu
from jax.sharding import PartitionSpec as P

D = 5120
RANK = 4
NORM_EPS = 1e-06
SIGMA_NOISE = 0.25
LEARN_RATE = 0.5
NX, NY, NZ = 4, 4, 8
ROWS = 64
FEAT = 640
WA, WB = 128, 256
VOC = 304
FACT = 128
F32, BF16 = jnp.float32, jnp.bfloat16
MESH_ID = pl.DeviceIdType.MESH
NT = (((1,), (1,)), ((), ()))


class Ids:
    def __init__(self):
        self.table = {}

    def __call__(self, *key):
        return self.table.setdefault(key, len(self.table))


SLOTS = {0: ("own", 0), 7: ("up", 4)}
for _s in (1, 2, 3):
    SLOTS[2 * _s - 1], SLOTS[2 * _s] = ("up", _s), ("dn", _s)
SLOT_OF = {where: k for k, where in SLOTS.items()}
SND = "snd"
RING = "z"
LAST = "y"
A = "A"
B = "B"
C = "C"
UP = "up"
DN = "dn"
OPP = "opp"
COMP = "comp"
RIGHT_Y = "Rtr"
RIGHT_X = "Rxr"
RIGHT_CORE = "Rdr"
HEAD = "head"
A_PLANE = "A2r"
FINE = (3, 4, 5, 6, 7)
ORDER = (
    (SND, LAST, B, 0, UP), (SND, LAST, B, 0, DN), (SND, RING, B, UP, 1),
    (SND, RING, B, DN, 1), (SND, LAST, C, 0, UP), (SND, LAST, C, 0, DN),
    (SND, RING, C, UP, 1), (SND, RING, C, DN, 1), (RIGHT_Y,), (HEAD,), (RING, B, UP, 1),
    (SND, LAST, B, 1, UP), (SND, LAST, B, 1, DN), (SND, RING, B, UP, 2), (LAST, B, 0, UP),
    (SND, LAST, B, 0, OPP), (LAST, C, 0, UP), (SND, LAST, C, 0, OPP), (LAST, B, 0, DN),
    (RING, B, DN, 1), (SND, RING, B, DN, 2), (SND, LAST, B, 2, UP), (SND, LAST, B, 2, DN),
    (LAST, C, 0, DN), (RING, C, UP, 1), (SND, LAST, C, 1, UP), (SND, LAST, C, 1, DN),
    (SND, RING, C, UP, 2), (RING, C, DN, 1), (SND, RING, C, DN, 2), (SND, LAST, C, 2, UP),
    (SND, LAST, C, 2, DN), (LAST, B, 1, UP), (SND, LAST, B, 1, OPP), (RING, B, UP, 2),
    (SND, RING, B, UP, 3), (SND, LAST, B, 3, UP), (SND, LAST, B, 3, DN), (A_PLANE,),
    (SND, RING, A, UP, 1), (SND, RING, A, DN, 1), (RING, B, DN, 2), (SND, RING, B, DN, 3),
    (SND, LAST, B, 4, UP), (SND, LAST, B, 4, DN), (LAST, B, 1, DN), (LAST, B, 0, OPP),
    (RING, C, UP, 2), (SND, RING, C, UP, 3), (SND, LAST, C, 3, UP), (SND, LAST, C, 3, DN),
    (RIGHT_X,), (LAST, B, 2, UP), (SND, LAST, B, 2, OPP), (RING, C, DN, 2), (SND, RING, C, DN, 3),
    (SND, LAST, C, 4, UP), (SND, LAST, C, 4, DN), (LAST, C, 0, OPP), (LAST, B, 2, DN),
    (RING, B, UP, 3), (SND, RING, B, UP, 4), (SND, LAST, B, 5, UP), (SND, LAST, B, 5, DN),
    (LAST, C, 1, UP), (SND, LAST, C, 1, OPP), (LAST, B, 1, OPP), (RIGHT_CORE,), (LAST, B, 3, UP),
    (SND, LAST, B, 3, OPP), (LAST, C, 1, DN), (RING, A, UP, 1), (SND, RING, A, UP, 2),
    (COMP, 0), (LAST, C, 2, UP), (SND, LAST, C, 2, OPP), (LAST, C, 2, DN), (LAST, B, 3, DN),
    (LAST, B, 4, UP), (SND, LAST, B, 4, OPP), (RING, A, DN, 1), (SND, RING, A, DN, 2),
    (LAST, C, 3, UP), (SND, LAST, C, 3, OPP), (LAST, B, 4, DN), (RING, B, DN, 3),
    (SND, LAST, B, 6, UP), (SND, LAST, B, 6, DN), (LAST, C, 3, DN), (LAST, B, 2, OPP),
    (RING, C, UP, 3), (SND, RING, C, UP, 4), (SND, LAST, C, 5, UP), (SND, LAST, C, 5, DN),
    (LAST, C, 4, UP), (SND, LAST, C, 4, OPP), (LAST, B, 5, UP), (SND, LAST, B, 5, OPP),
    (RING, C, DN, 3), (SND, LAST, C, 6, UP), (SND, LAST, C, 6, DN), (LAST, C, 4, DN),
    (LAST, B, 5, DN), (RING, B, UP, 4), (SND, LAST, B, 7, UP), (SND, LAST, B, 7, DN),
    (LAST, C, 1, OPP), (LAST, B, 3, OPP), (LAST, C, 2, OPP), (LAST, B, 4, OPP), (RING, A, UP, 2),
    (SND, RING, A, UP, 3), (COMP, 1), (LAST, B, 6, UP), (SND, LAST, B, 6, OPP),
    (LAST, C, 5, UP), (SND, LAST, C, 5, OPP), (LAST, C, 3, OPP), (LAST, B, 6, DN),
    (RING, A, DN, 2), (SND, RING, A, DN, 3), (COMP, 2), (RING, C, UP, 4),
    (SND, LAST, C, 7, UP), (SND, LAST, C, 7, DN), (LAST, C, 4, OPP), (LAST, B, 5, OPP),
    (LAST, B, 7, UP), (SND, LAST, B, 7, OPP), (LAST, C, 5, DN), (COMP, 3), (LAST, C, 6, UP),
    (SND, LAST, C, 6, OPP), (LAST, C, 6, DN), (LAST, B, 7, DN), (LAST, B, 6, OPP),
    (RING, A, UP, 3), (SND, RING, A, UP, 4), (COMP, 4), (LAST, C, 7, UP),
    (SND, LAST, C, 7, OPP), (LAST, C, 5, OPP), (LAST, B, 7, OPP), (RING, A, DN, 3),
    (LAST, C, 7, DN), (LAST, C, 6, OPP), (COMP, 5), (LAST, C, 7, OPP), (RING, A, UP, 4),
    (COMP, 6), (COMP, 7),
)


def message_names():
    ids = Ids()
    for dx in range(4):
        for dy in range(4):
            ids("sq", dx, dy)
    for d in range(1, 4):
        for kind in ("Rt", "B1", "C1", "A1", "A2"):
            ids(kind, d)
    ids("Rx")
    ids("Rd")
    for part in "ABC":
        for s in range(1, 5):
            ids("z", part, "up", s)
            if s < 4:
                ids("z", part, "dn", s)
    for k in range(8):
        for part in "BC":
            for way in ("up", "dn", "opp"):
                ids("last", part, k, way)
        for part in "ABC":
            if part != "A" and k in FINE:
                for piece in range(4):
                    ids("core", part, k, piece)
            else:
                ids("core", part, k)
    for i in range(2):
        for k in range(8):
            ids("stat1", i, k)
            ids("stat3", i, k)
            ids("stat2", i, k)
    return ids


IDS = message_names()
N_MSG = len(IDS.table)


def combine(stats):
    top = stats[:, 0, :]
    best = jnp.max(top, axis=0, keepdims=True)
    total = jnp.sum(stats[:, 1, :] * jnp.exp(top - best), axis=0, keepdims=True)
    target = jnp.sum(stats[:, 2, :], axis=0, keepdims=True)
    return best, total, target


def gather_kernel(
    hid_in, gain_in, right_in, left_in, tgt_in, master_ref,
    out_ref, stage, rt,
    hid_ref, gain_ref, right_ref, left_ref, tgt_ref, buf_a, buf_b, buf_c, head, slot_right, acc, raw_a, raw_b, raw_c, sq, st, r1, r2, r3,
    ssem, rsem, lsem,
):
    pop, tp = lax.axis_index("pop"), lax.axis_index("tp")
    c = lax.rem(pop, 2)
    z = lax.rem(lax.div(pop, 2), NZ)
    x_lo = lax.div(pop, 2 * NZ)
    x_hi = lax.div(tp, NY)
    y = lax.rem(tp, NY)
    x = x_hi * 2 + x_lo
    sib = 1 - c
    sgn = 1 - 2 * c
    blk = x_lo * NZ + z
    quad = c * 8 + tp

    xs = [lax.rem(x + k, NX) for k in range(NX)]
    ys = [lax.rem(y + k, NY) for k in range(NY)]
    zs = {k: lax.rem(z + k * sgn + NZ, NZ) for k in range(-4, 8)}
    xo = {k: lax.rem(x + k * sgn + NX, NX) for k in (-1, 0, 1, 2)}
    yo = {k: lax.rem(y + k * sgn + NY, NY) for k in (-1, 0, 1, 2)}
    los = (x_lo, 1 - x_lo)

    def dev(xx, yy, zz, cc):
        return ((lax.rem(xx, 2) * NZ + zz) * 2 + cc, lax.div(xx, 2) * NY + yy)

    sent = []

    def send(key, src, dst, device):
        i = IDS(*key)
        copy = pltpu.make_async_remote_copy(
            src_ref=src, dst_ref=dst, send_sem=ssem.at[i], recv_sem=rsem.at[i],
            device_id=device, device_id_type=MESH_ID,
        )
        copy.start()
        sent.append(copy)

    def recv(key, dst, device):
        i = IDS(*key)
        pltpu.make_async_remote_copy(
            src_ref=dst, dst_ref=dst, send_sem=ssem.at[i], recv_sem=rsem.at[i],
            device_id=device, device_id_type=MESH_ID,
        ).wait_recv()

    mirror = dev(3 - x, y, z, c)
    sibling = dev(x, y, z, sib)

    def plane(dx, dy):
        return dev(xs[dx], ys[dy], z, c)

    far = (2, 1, 3, 0)
    PLANE = [(dx, dy) for dx in far for dy in far if dx or dy]

    barrier = pltpu.get_barrier_semaphore()
    for dx, dy in PLANE:
        pl.semaphore_signal(barrier, inc=1, device_id=plane(dx, dy), device_id_type=MESH_ID)
    for device in (dev(x, y, zs[1], c), dev(x, y, zs[-1], c), sibling):
        pl.semaphore_signal(barrier, inc=1, device_id=device, device_id_type=MESH_ID)

    loads = [
        pltpu.make_async_copy(src, dst, lsem.at[i])
        for i, (src, dst) in enumerate(
            (
                (hid_in, hid_ref), (gain_in, gain_ref), (right_in, right_ref),
                (left_in, left_ref), (tgt_in, tgt_ref), (master_ref, stage),
            )
        )
    ]
    for load in loads:
        load.start()
    loads[0].wait()

    raw_a[pl.ds(x, 1)] = hid_ref[:, :WA][None]
    raw_b[pl.ds(x, 1)] = hid_ref[:, WA:WA + WB][None]
    raw_c[pl.ds(y, 1)] = hid_ref[:, WA + WB:][None]
    folded = jnp.zeros((ROWS, 128), F32)
    for j in range(FEAT // 128):
        piece = hid_ref[:, j * 128:(j + 1) * 128].astype(F32)
        folded = folded + piece * piece
    folded = jnp.concatenate([folded, jnp.zeros((128 - ROWS, 128), F32)], axis=0)
    row_sq = jnp.sum(folded.T, axis=0, keepdims=True)
    loads[1].wait()
    gains = [gain_ref[pl.ds(j * 128, 128)].reshape(1, 128) for j in range(FEAT // 128)]
    packed = jnp.concatenate([row_sq] + gains + [jnp.zeros((2, 128), F32)], axis=0)
    sq[pl.ds(x, 1), pl.ds(y, 1)] = packed[None, None]
    pl.semaphore_wait(barrier, len(PLANE) + 3)

    for dx, dy in PLANE:
        send(("sq", dx, dy), sq.at[x, y], sq.at[x, y], plane(dx, dy))
    for d in (2, 1, 3):
        send(("B1", d), raw_b.at[x], raw_b.at[x], plane(d, 0))
        send(("C1", d), raw_c.at[y], raw_c.at[y], plane(0, d))
    for d in (1, 3, 2):
        send(("A1", d), raw_a.at[x], raw_a.at[x], plane(d, 0))
    loads[2].wait()
    for j in range(FEAT // 128):
        block_t = right_ref[j * 128:(j + 1) * 128, :].astype(F32).T.astype(BF16)
        rt[c, pl.ds(tp, 1), :, j * 128:(j + 1) * 128] = jnp.where(c == 0, block_t[:64], block_t[64:])[None]
    for d in (1, 3, 2):
        send(("Rt", d), rt.at[c, tp], rt.at[c, tp], plane(0, d))

    def z_dev(k):
        return dev(x, y, zs[k], c)

    def y_dev(k):
        return dev(x, yo[k], z, c)

    def x_dev(k):
        return dev(xo[k], y, z, c)

    def blk_a(zz):
        return buf_a.at[zz, c]

    def blk_b(zz, yy):
        return buf_b.at[zz, c, yy]

    def blk_c(zz, xx):
        return buf_c.at[zz, c, xx]

    def z_blk(part, zz):
        return blk_a(zz) if part == "A" else blk_b(zz, y) if part == "B" else blk_c(zz, x)

    def slot_z(way, s, orient=1):
        return zs[-orient * s if way == "up" else orient * s]

    def hand_over(part, k, zz):
        if k in FINE:
            send(("core", part, k, 0), z_blk(part, zz), z_blk(part, zz), sibling)

    def last_blk(part, zz, k):
        return blk_b(zz, yo[k]) if part == "B" else blk_c(zz, xo[k])

    def ring_send(part, way, s):
        block = z_blk(part, slot_z(way, s - 1))
        send(("z", part, way, s), block, block, z_dev(1 if way == "up" else -1))

    def last_send(part, k, way):
        zz = slot_z(*SLOTS[k])
        block = last_blk(part, zz, -1 if way == "opp" else 0)
        there = y_dev if part == "B" else x_dev
        send(("last", part, k, way), block, block, there(-1 if way == "dn" else 1))

    def take_z(part, way, s):
        k = SLOT_OF[way, s]
        zz = slot_z(way, s)
        block = z_blk(part, zz)
        recv(("z", part, way, s), block, z_dev(-1 if way == "up" else 1))
        if part == "A":
            send(("core", "A", k), block, block, sibling)
        else:
            hand_over(part, k, zz)

    pieces_in = {}

    def take_last(part, k, way):
        zz = slot_z(*SLOTS[k])
        there = y_dev if part == "B" else x_dev
        block = last_blk(part, zz, {"up": -1, "dn": 1, "opp": 2}[way])
        recv(("last", part, k, way), block, there(1 if way == "dn" else -1))
        if k in FINE:
            send(("core", part, k, {"up": 1, "dn": 2, "opp": 3}[way]), block, block, sibling)
        else:
            pieces_in[part, k] = pieces_in.get((part, k), 0) + 1
            if pieces_in[part, k] == 3:
                whole = (buf_b if part == "B" else buf_c).at[zz, c]
                send(("core", part, k), whole, whole, sibling)

    def core_recv(k, zz):
        recv(("core", "A", k), buf_a.at[zz, sib], sibling)
        for part, ref, other in (("B", buf_b, yo), ("C", buf_c, xo)):
            if k in FINE:
                for piece, at in ((0, 0), (1, 1), (2, -1), (3, 2)):
                    recv(("core", part, k, piece), ref.at[zz, sib, other[at]], sibling)
            else:
                recv(("core", part, k), ref.at[zz, sib], sibling)

    def by_part(t):
        hi_t = t // NY
        yield slice(0, WA), slice(hi_t * WA, (hi_t + 1) * WA)
        for i in range(2):
            start = 2 * WA + (2 * i + hi_t) * WB
            yield slice(WA + i * WB, WA + (i + 1) * WB), slice(start, start + WB)

    def fill_head():
        for t in range(8):
            for source, place in by_part(t):
                columns = slice(t * FEAT + source.start, t * FEAT + source.stop)
                head[t % NY, :, place] = stage[:, columns].astype(BF16)

    def fill_right():
        for t in range(8):
            halves = [rt[half, t].astype(F32) for half in range(2)]
            for zz in range(NZ):
                rows = slice(8 * zz, 8 * zz + 8)
                both = jnp.concatenate([half[rows] for half in halves], axis=0).astype(BF16)
                for source, place in by_part(t):
                    slot_right[zz, t % NY, :, place] = both[:, source]

    offset = (pop * 8 + tp) * VOC

    def compute_one(zz):
        def tokens(piece, hi):
            return jnp.concatenate([piece(cc, hi * 2 + lo) for lo in range(2) for cc in range(2)], axis=0)

        def features(yy, carry):
            columns = [tokens(lambda cc, xx: buf_a[zz, cc, yy, xx], hi) for hi in range(2)]
            columns += [tokens(lambda cc, xx: buf_b[zz, cc, yy, xx], hi) for hi in range(2)]
            columns += [tokens(lambda cc, xx: buf_c[zz, cc, xx, yy], hi) for hi in range(2)]
            acc[...] += lax.dot_general(
                jnp.concatenate([head[yy], slot_right[zz, yy]], axis=0),
                jnp.concatenate(columns, axis=1), NT, preferred_element_type=F32,
            )
            return carry

        acc[...] = jnp.zeros((VOC + 16, 256), F32)
        lax.fori_loop(0, NY, features, 0)
        full = acc[...]
        lane = lax.broadcasted_iota(jnp.int32, (16, 256), 1)
        column = lax.broadcasted_iota(jnp.int32, (16, 256), 0)
        own = lax.shift_right_logical(column, 2) == lax.shift_right_logical(lane, 6)
        odd = lax.bitwise_and(lax.shift_right_logical(lane, 5), 1)
        sign = jnp.where(odd == 0, SIGMA_NOISE, -SIGMA_NOISE)
        few = jnp.where(own, full[VOC:] * sign, 0.0)
        spread = jnp.concatenate([few[:8]] * NZ + [few[8:]] * NZ, axis=0)
        place = lax.broadcasted_iota(jnp.int32, (FACT, 256), 0)
        here = lax.bitwise_and(lax.shift_right_logical(place, 3), NZ - 1) == zz
        lowrank = jnp.where(here, spread, 0.0).astype(BF16)
        logits = full[:VOC] + jnp.dot(left_ref[...], lowrank, preferred_element_type=F32)
        best = jnp.max(logits, axis=0, keepdims=True)
        total = jnp.sum(jnp.exp(logits - best), axis=0, keepdims=True)
        wanted = jnp.concatenate([tgt_ref[zz], tgt_ref[NZ + zz]], axis=1) - offset
        rows = lax.broadcasted_iota(jnp.int32, (VOC, 256), 0)
        target = jnp.sum(jnp.where(rows == wanted, logits, 0.0), axis=0, keepdims=True)
        packed = jnp.concatenate([best, total, target, jnp.zeros((5, 256), F32)], axis=0)
        st[zz, 0] = packed[:, :128]
        st[zz, 1] = packed[:, 128:]

    def stat_send(k):
        for i in range(2):
            if i or k:
                send(("stat1", i, k), st.at[zs[(k + 4) % 8], los[i]], r1.at[blk], dev(x_hi * 2 + los[i], y, zs[k], c))

    def compute(k):
        way, s = SLOTS[k]
        zz = slot_z(way, s, -1)
        core_recv(k, zz)
        compute_one(zz)
        stat_send(((8 - s if way == "dn" else s) + 4) % 8)

    def step(what, *which):
        if what == "snd":
            (ring_send if which[0] == "z" else last_send)(*which[1:])
        elif what == "z":
            take_z(*which)
        elif what == "y":
            take_last(*which)
        elif what == "comp":
            compute(*which)
        elif what == "head":
            for load in loads[3:]:
                load.wait()
            fill_head()
        elif what == "A2r":
            for d in (1, 3, 2):
                recv(("A2", d), buf_a.at[z, c, ys[-d]], plane(0, -d))
            send(("core", "A", 0), blk_a(z), blk_a(z), sibling)
        elif what == "Rtr":
            for d in range(1, 4):
                recv(("Rt", d), rt.at[c, x_hi * NY + ys[-d]], plane(0, -d))
            send(("Rx",), rt.at[c, pl.ds(x_hi * NY, NY)], rt.at[c, pl.ds(x_hi * NY, NY)], mirror)
        elif what == "Rxr":
            recv(("Rx",), rt.at[c, pl.ds((1 - x_hi) * NY, NY)], mirror)
            send(("Rd",), rt.at[c], rt.at[c], sibling)
        else:
            recv(("Rd",), rt.at[sib], sibling)
            fill_right()

    def follow(first, part):
        at = first
        while at < len(ORDER):
            action = ORDER[at]
            if part is not None and not (action[0] == "snd" and action[2] == part):
                break
            step(*action)
            at += 1
        return at

    for dx, dy in PLANE:
        recv(("sq", dx, dy), sq.at[xs[-dx], ys[-dy]], plane(-dx, -dy))
    scales = []
    for lo in range(2):
        total = sq[lo, :, 0, :] + sq[lo + 2, :, 0, :]
        row_scale = lax.rsqrt(jnp.sum(total, axis=0, keepdims=True) / D + NORM_EPS)
        scales.append(jnp.broadcast_to(row_scale, (128, 128)).T[:ROWS, :])
    own_scale = jnp.where(x_lo == 0, scales[0], scales[1])

    def normalize(values, scale, xx, yy, first, count):
        return jnp.concatenate(
            [
                (values[:, j * 128:(j + 1) * 128].astype(F32) * scale * sq[xx, yy, 1 + first + j:2 + first + j, :]).astype(BF16)
                for j in range(count)
            ],
            axis=1,
        )

    for d in (1, 3, 2):
        recv(("B1", d), raw_b.at[xs[-d]], plane(-d, 0))
    for t in range(NX):
        buf_b[z, c, y, t] = normalize(raw_b[t], scales[t % 2], t, y, 1, 2)
    hand_over("B", 0, z)
    start_from = follow(0, "B")
    for d in (1, 3, 2):
        recv(("C1", d), raw_c.at[ys[-d]], plane(0, -d))
    for t in range(NY):
        buf_c[z, c, x, t] = normalize(raw_c[t], own_scale, x, t, 3, 2)
    hand_over("C", 0, z)
    start_from = follow(start_from, "C")
    for d in (1, 3, 2):
        recv(("A1", d), raw_a.at[xs[-d]], plane(-d, 0))
    for t in range(NX):
        buf_a[z, c, y, t] = normalize(raw_a[t], scales[t % 2], t, y, 0, 1)
    for d in (1, 3, 2):
        send(("A2", d), buf_a.at[z, c, y], buf_a.at[z, c, y], plane(0, d))

    follow(start_from, None)

    r1[pl.ds(blk, 1)] = st[zs[4], x_lo][None]
    for copy in sent:
        copy.wait_send()
    sent.clear()
    for k in range(8):
        for i in range(2):
            if i or k:
                recv(("stat1", i, k), r1.at[los[i] * NZ + zs[-k if k < 5 else 8 - k]], dev(x_hi * 2 + los[i], y, zs[-k if k < 5 else 8 - k], c))
    best, total, target = combine(r1[...])
    packed = jnp.concatenate([best, total, target, jnp.zeros((5, 128), F32)], axis=0)
    r2[pl.ds(quad, 1)] = packed[None]

    def quad_at(i, k):
        h, d = divmod(k, 4)
        hi = x_hi if h == 0 else 1 - x_hi
        cc = c if i == 0 else sib
        return cc, hi, d

    QUAD = [(i, k) for i in (1, 0) for k in (6, 2, 5, 7, 1, 3, 4, 0) if i or k]
    RING = [(i, k) for i in (1, 0) for k in (4, 3, 5, 2, 6, 1, 7, 0) if i or k]
    for i, k in QUAD:
        cc, hi, d = quad_at(i, k)
        send(("stat2", i, k), r2.at[quad], r2.at[quad], dev(hi * 2 + x_lo, ys[d], z, cc))
    for i, k in QUAD:
        cc, hi, d = quad_at(i, k)
        recv(("stat2", i, k), r2.at[cc * 8 + hi * NY + ys[-d]], dev(hi * 2 + x_lo, ys[-d], z, cc))
    best, total, target = combine(r2[...])
    logprob = target - best - jnp.log(total)
    lane = lax.broadcasted_iota(jnp.int32, (1, 128), 1)
    zero = jnp.zeros((1, 128), F32)
    means = [
        jnp.sum(jnp.where(lax.shift_right_logical(lane, 5) == m, logprob, 0.0), axis=1, keepdims=True) / 32.0
        for m in range(4)
    ]
    loglik, weights = zero, zero
    owned = x_lo * NZ + zs[4]
    for m in range(4):
        loglik = jnp.where(lane == owned * 4 + m, means[m], loglik)
    for h in range(2):
        weights = jnp.where(lax.shift_right_logical(lane, 2) == owned * 2 + h, means[2 * h] - means[2 * h + 1], weights)
    packed = jnp.concatenate([loglik, weights, jnp.zeros((6, 128), F32)], axis=0)
    r3[pl.ds(blk, 1)] = packed[None]
    for i, k in RING:
        send(("stat3", i, k), r3.at[blk], r3.at[blk], dev(x_hi * 2 + los[i], y, zs[k], c))
    for i, k in RING:
        zz = zs[-k if k < 5 else 8 - k]
        recv(("stat3", i, k), r3.at[los[i] * NZ + zz], dev(x_hi * 2 + los[i], y, zz, c))
    out_ref[...] = jnp.sum(r3[...], axis=0)
    for copy in sent:
        copy.wait_send()


def update_kernel(w_ref, left_ref, rt_ref, master_ref, ll_ref, out_ref, block, sems):
    ll_ref[...] = w_ref[0, :64]
    scaled = (left_ref[...].astype(F32) * w_ref[1:2, :]).astype(BF16)
    copies = []
    for t in range(8):
        cols = slice(t * FEAT, (t + 1) * FEAT)
        right = jnp.concatenate([rt_ref[0, t], rt_ref[1, t]], axis=0)
        update = jnp.dot(scaled, right, preferred_element_type=F32)
        block[:, cols] = master_ref[:, cols] + LEARN_RATE * update
        copy = pltpu.make_async_copy(block.at[:, cols], out_ref.at[:, cols], sems.at[t])
        copy.start()
        copies.append(copy)
    for copy in copies:
        copy.wait()


def body(hidden, norm_gain, right_factors, left_factors, targets, master):
    vmem = pl.BlockSpec(memory_space=pltpu.VMEM)
    hbm = pl.BlockSpec(memory_space=pl.ANY)
    result, stage, right_t = pl.pallas_call(
        gather_kernel,
        out_shape=(
            pltpu.VMEM((8, 128), F32),
            pltpu.VMEM((VOC, D), F32),
            pltpu.VMEM((2, 8, 64, FEAT), BF16),
        ),
        in_specs=[hbm] * 6,
        out_specs=(vmem, vmem, vmem),
        scratch_shapes=[
            pltpu.VMEM((ROWS, FEAT), BF16),
            pltpu.VMEM((FEAT,), F32),
            pltpu.VMEM((FEAT, FACT), BF16),
            pltpu.VMEM((VOC, FACT), BF16),
            pltpu.VMEM((16, 1, 128), jnp.int32),
            pltpu.VMEM((NZ, 2, NY, NX, ROWS, WA), BF16),
            pltpu.VMEM((NZ, 2, NY, NX, ROWS, WB), BF16),
            pltpu.VMEM((NZ, 2, NX, NY, ROWS, WB), BF16),
            pltpu.VMEM((NY, VOC, 2 * FEAT), BF16),
            pltpu.VMEM((NZ, NY, 16, 2 * FEAT), BF16),
            pltpu.VMEM((VOC + 16, 256), F32),
            pltpu.VMEM((NX, ROWS, WA), BF16),
            pltpu.VMEM((NX, ROWS, WB), BF16),
            pltpu.VMEM((NY, ROWS, WB), BF16),
            pltpu.VMEM((NX, NY, 8, 128), F32),
            pltpu.VMEM((NZ, 2, 8, 128), F32),
            pltpu.VMEM((16, 8, 128), F32),
            pltpu.VMEM((16, 8, 128), F32),
            pltpu.VMEM((16, 8, 128), F32),
            pltpu.SemaphoreType.DMA((N_MSG,)),
            pltpu.SemaphoreType.DMA((N_MSG,)),
            pltpu.SemaphoreType.DMA((6,)),
        ],
        compiler_params=pltpu.CompilerParams(
            collective_id=0, has_side_effects=True, vmem_limit_bytes=52 * 1024 * 1024
        ),
        name="gather_logits",
    )(
        hidden, norm_gain, right_factors, left_factors,
        targets.reshape(16, 1, 128), master,
    )
    loglik, new_master = pl.pallas_call(
        update_kernel,
        out_shape=(jax.ShapeDtypeStruct((64,), F32), jax.ShapeDtypeStruct((VOC, D), F32)),
        in_specs=[vmem, vmem, vmem, vmem],
        out_specs=(vmem, hbm),
        scratch_shapes=[pltpu.VMEM((VOC, D), F32), pltpu.SemaphoreType.DMA((8,))],
        compiler_params=pltpu.CompilerParams(vmem_limit_bytes=20 * 1024 * 1024),
        name="update_master",
    )(result, left_factors, right_t, stage)
    return (loglik, new_master)


def solution(mesh):
    in_specs = (
        P("pop", "tp"),
        P("tp"),
        P("tp", None),
        P(("pop", "tp"), None),
        P(),
        P(("pop", "tp"), None),
    )
    out_specs = (P(), P(("pop", "tp"), None))
    return jax.shard_map(body, mesh=mesh, in_specs=in_specs, out_specs=out_specs, check_vma=False)
```

```python
import jax
import jax.numpy as jnp
from jax import lax
from jax.experimental import pallas as pl
from jax.experimental.pallas import tpu as pltpu
from jax.sharding import PartitionSpec as P

D = 5120
RANK = 4
NORM_EPS = 1e-06
SIGMA_NOISE = 0.25
LEARN_RATE = 0.5
NX, NY, NZ = 4, 4, 8
ROWS = 64
FEAT = 640
WA, WB = 128, 256
VOC = 304
FACT = 128
F32, BF16 = jnp.float32, jnp.bfloat16
MESH_ID = pl.DeviceIdType.MESH
NT = (((1,), (1,)), ((), ()))


class Ids:
    def __init__(self):
        self.table = {}

    def __call__(self, *key):
        return self.table.setdefault(key, len(self.table))


SLOTS = {0: ("own", 0), 7: ("up", 4)}
for _s in (1, 2, 3):
    SLOTS[2 * _s - 1], SLOTS[2 * _s] = ("up", _s), ("dn", _s)
SLOT_OF = {where: k for k, where in SLOTS.items()}
SND = "snd"
RING = "z"
LAST = "y"
A = "A"
B = "B"
C = "C"
UP = "up"
DN = "dn"
OPP = "opp"
COMP = "comp"
RIGHT_Y = "Rtr"
RIGHT_X = "Rxr"
RIGHT_CORE = "Rdr"
HEAD = "head"
A_PLANE = "A2r"
FINE = (3, 4, 5, 6, 7)
ORDER = (
    (SND, LAST, B, 0, UP), (SND, LAST, B, 0, DN), (SND, RING, B, UP, 1),
    (SND, RING, B, DN, 1), (SND, LAST, C, 0, UP), (SND, LAST, C, 0, DN),
    (SND, RING, C, UP, 1), (SND, RING, C, DN, 1), (RIGHT_Y,), (HEAD,), (RING, B, UP, 1),
    (SND, LAST, B, 1, UP), (SND, LAST, B, 1, DN), (SND, RING, B, UP, 2), (LAST, B, 0, UP),
    (SND, LAST, B, 0, OPP), (LAST, C, 0, UP), (SND, LAST, C, 0, OPP), (LAST, B, 0, DN),
    (RING, B, DN, 1), (SND, RING, B, DN, 2), (SND, LAST, B, 2, UP), (SND, LAST, B, 2, DN),
    (LAST, C, 0, DN), (RING, C, UP, 1), (SND, LAST, C, 1, UP), (SND, LAST, C, 1, DN),
    (SND, RING, C, UP, 2), (RING, C, DN, 1), (SND, RING, C, DN, 2), (SND, LAST, C, 2, UP),
    (SND, LAST, C, 2, DN), (LAST, B, 1, UP), (SND, LAST, B, 1, OPP), (RING, B, UP, 2),
    (SND, RING, B, UP, 3), (SND, LAST, B, 3, UP), (SND, LAST, B, 3, DN), (A_PLANE,),
    (SND, RING, A, UP, 1), (SND, RING, A, DN, 1), (RING, B, DN, 2), (SND, RING, B, DN, 3),
    (SND, LAST, B, 4, UP), (SND, LAST, B, 4, DN), (LAST, B, 1, DN), (LAST, B, 0, OPP),
    (RING, C, UP, 2), (SND, RING, C, UP, 3), (SND, LAST, C, 3, UP), (SND, LAST, C, 3, DN),
    (RIGHT_X,), (LAST, B, 2, UP), (SND, LAST, B, 2, OPP), (RING, C, DN, 2), (SND, RING, C, DN, 3),
    (SND, LAST, C, 4, UP), (SND, LAST, C, 4, DN), (LAST, C, 0, OPP), (LAST, B, 2, DN),
    (RING, B, UP, 3), (SND, RING, B, UP, 4), (SND, LAST, B, 5, UP), (SND, LAST, B, 5, DN),
    (LAST, C, 1, UP), (SND, LAST, C, 1, OPP), (LAST, B, 1, OPP), (RIGHT_CORE,), (LAST, B, 3, UP),
    (SND, LAST, B, 3, OPP), (LAST, C, 1, DN), (RING, A, UP, 1), (SND, RING, A, UP, 2),
    (COMP, 0), (LAST, C, 2, UP), (SND, LAST, C, 2, OPP), (LAST, B, 3, DN), (LAST, C, 2, DN),
    (LAST, B, 4, UP), (SND, LAST, B, 4, OPP), (RING, A, DN, 1), (SND, RING, A, DN, 2),
    (LAST, C, 3, UP), (SND, LAST, C, 3, OPP), (LAST, B, 4, DN), (RING, B, DN, 3),
    (SND, LAST, B, 6, UP), (SND, LAST, B, 6, DN), (LAST, C, 3, DN), (LAST, B, 2, OPP),
    (RING, C, UP, 3), (SND, RING, C, UP, 4), (SND, LAST, C, 5, UP), (SND, LAST, C, 5, DN),
    (LAST, C, 4, UP), (SND, LAST, C, 4, OPP), (LAST, B, 5, UP), (SND, LAST, B, 5, OPP),
    (RING, C, DN, 3), (SND, LAST, C, 6, UP), (SND, LAST, C, 6, DN), (LAST, C, 4, DN),
    (LAST, B, 5, DN), (RING, B, UP, 4), (SND, LAST, B, 7, UP), (SND, LAST, B, 7, DN),
    (LAST, C, 1, OPP), (LAST, B, 3, OPP), (LAST, C, 2, OPP), (LAST, B, 4, OPP), (RING, A, UP, 2),
    (SND, RING, A, UP, 3), (COMP, 1), (LAST, B, 6, UP), (SND, LAST, B, 6, OPP),
    (LAST, C, 3, OPP), (LAST, C, 5, UP), (SND, LAST, C, 5, OPP), (COMP, 2), (LAST, B, 6, DN),
    (LAST, C, 5, DN), (RING, A, DN, 2), (SND, RING, A, DN, 3), (LAST, B, 5, OPP),
    (RING, C, UP, 4), (SND, LAST, C, 7, UP), (SND, LAST, C, 7, DN), (LAST, C, 4, OPP),
    (COMP, 3), (LAST, C, 6, UP), (SND, LAST, C, 6, OPP), (LAST, B, 7, UP),
    (SND, LAST, B, 7, OPP), (LAST, B, 7, DN), (COMP, 4), (LAST, B, 6, OPP), (LAST, C, 6, DN),
    (RING, A, UP, 3), (SND, RING, A, UP, 4), (LAST, C, 5, OPP), (RING, A, DN, 3),
    (LAST, C, 7, UP), (SND, LAST, C, 7, OPP), (LAST, B, 7, OPP), (LAST, C, 7, DN),
    (LAST, C, 6, OPP), (COMP, 5), (LAST, C, 7, OPP), (RING, A, UP, 4), (COMP, 6), (COMP, 7),
)


def message_names():
    ids = Ids()
    for dx in range(4):
        for dy in range(4):
            ids("sq", dx, dy)
    for d in range(1, 4):
        for kind in ("Rt", "B1", "C1", "A1", "A2"):
            ids(kind, d)
    ids("Rx")
    ids("Rd")
    for part in "ABC":
        for s in range(1, 5):
            ids("z", part, "up", s)
            if s < 4:
                ids("z", part, "dn", s)
    for k in range(8):
        for part in "BC":
            for way in ("up", "dn", "opp"):
                ids("last", part, k, way)
        for part in "ABC":
            if part != "A" and k in FINE:
                for piece in range(4):
                    ids("core", part, k, piece)
            else:
                ids("core", part, k)
    for i in range(2):
        for k in range(8):
            ids("stat1", i, k)
            ids("stat3", i, k)
            ids("stat2", i, k)
    return ids


IDS = message_names()
N_MSG = len(IDS.table)


def combine(stats):
    top = stats[:, 0, :]
    best = jnp.max(top, axis=0, keepdims=True)
    total = jnp.sum(stats[:, 1, :] * jnp.exp(top - best), axis=0, keepdims=True)
    target = jnp.sum(stats[:, 2, :], axis=0, keepdims=True)
    return best, total, target


def gather_kernel(
    hid_in, gain_in, right_in, left_in, tgt_in, master_ref,
    out_ref, stage, rt,
    hid_ref, gain_ref, right_ref, left_ref, tgt_ref, buf_a, buf_b, buf_c, head, slot_right, acc, raw_a, raw_b, raw_c, sq, st, r1, r2, r3,
    ssem, rsem, lsem,
):
    pop, tp = lax.axis_index("pop"), lax.axis_index("tp")
    c = lax.rem(pop, 2)
    z = lax.rem(lax.div(pop, 2), NZ)
    x_lo = lax.div(pop, 2 * NZ)
    x_hi = lax.div(tp, NY)
    y = lax.rem(tp, NY)
    x = x_hi * 2 + x_lo
    sib = 1 - c
    sgn = 1 - 2 * c
    blk = x_lo * NZ + z
    quad = c * 8 + tp

    xs = [lax.rem(x + k, NX) for k in range(NX)]
    ys = [lax.rem(y + k, NY) for k in range(NY)]
    zs = {k: lax.rem(z + k * sgn + NZ, NZ) for k in range(-4, 8)}
    xo = {k: lax.rem(x + k * sgn + NX, NX) for k in (-1, 0, 1, 2)}
    yo = {k: lax.rem(y + k * sgn + NY, NY) for k in (-1, 0, 1, 2)}
    los = (x_lo, 1 - x_lo)

    def dev(xx, yy, zz, cc):
        return ((lax.rem(xx, 2) * NZ + zz) * 2 + cc, lax.div(xx, 2) * NY + yy)

    sent = []

    def send(key, src, dst, device):
        i = IDS(*key)
        copy = pltpu.make_async_remote_copy(
            src_ref=src, dst_ref=dst, send_sem=ssem.at[i], recv_sem=rsem.at[i],
            device_id=device, device_id_type=MESH_ID,
        )
        copy.start()
        sent.append(copy)

    def recv(key, dst, device):
        i = IDS(*key)
        pltpu.make_async_remote_copy(
            src_ref=dst, dst_ref=dst, send_sem=ssem.at[i], recv_sem=rsem.at[i],
            device_id=device, device_id_type=MESH_ID,
        ).wait_recv()

    mirror = dev(3 - x, y, z, c)
    sibling = dev(x, y, z, sib)

    def plane(dx, dy):
        return dev(xs[dx], ys[dy], z, c)

    far = (2, 1, 3, 0)
    PLANE = [(dx, dy) for dx in far for dy in far if dx or dy]

    barrier = pltpu.get_barrier_semaphore()
    for dx, dy in PLANE:
        pl.semaphore_signal(barrier, inc=1, device_id=plane(dx, dy), device_id_type=MESH_ID)
    for device in (dev(x, y, zs[1], c), dev(x, y, zs[-1], c), sibling):
        pl.semaphore_signal(barrier, inc=1, device_id=device, device_id_type=MESH_ID)

    loads = [
        pltpu.make_async_copy(src, dst, lsem.at[i])
        for i, (src, dst) in enumerate(
            (
                (hid_in, hid_ref), (gain_in, gain_ref), (right_in, right_ref),
                (left_in, left_ref), (tgt_in, tgt_ref), (master_ref, stage),
            )
        )
    ]
    for load in loads:
        load.start()
    loads[0].wait()

    raw_a[pl.ds(x, 1)] = hid_ref[:, :WA][None]
    raw_b[pl.ds(x, 1)] = hid_ref[:, WA:WA + WB][None]
    raw_c[pl.ds(y, 1)] = hid_ref[:, WA + WB:][None]
    folded = jnp.zeros((ROWS, 128), F32)
    for j in range(FEAT // 128):
        piece = hid_ref[:, j * 128:(j + 1) * 128].astype(F32)
        folded = folded + piece * piece
    folded = jnp.concatenate([folded, jnp.zeros((128 - ROWS, 128), F32)], axis=0)
    row_sq = jnp.sum(folded.T, axis=0, keepdims=True)
    loads[1].wait()
    gains = [gain_ref[pl.ds(j * 128, 128)].reshape(1, 128) for j in range(FEAT // 128)]
    packed = jnp.concatenate([row_sq] + gains + [jnp.zeros((2, 128), F32)], axis=0)
    sq[pl.ds(x, 1), pl.ds(y, 1)] = packed[None, None]
    pl.semaphore_wait(barrier, len(PLANE) + 3)

    for dx, dy in PLANE:
        send(("sq", dx, dy), sq.at[x, y], sq.at[x, y], plane(dx, dy))
    for d in (2, 1, 3):
        send(("B1", d), raw_b.at[x], raw_b.at[x], plane(d, 0))
        send(("C1", d), raw_c.at[y], raw_c.at[y], plane(0, d))
    for d in (1, 3, 2):
        send(("A1", d), raw_a.at[x], raw_a.at[x], plane(d, 0))
    loads[2].wait()
    for j in range(FEAT // 128):
        block_t = right_ref[j * 128:(j + 1) * 128, :].astype(F32).T.astype(BF16)
        rt[c, pl.ds(tp, 1), :, j * 128:(j + 1) * 128] = jnp.where(c == 0, block_t[:64], block_t[64:])[None]
    for d in (1, 3, 2):
        send(("Rt", d), rt.at[c, tp], rt.at[c, tp], plane(0, d))

    def z_dev(k):
        return dev(x, y, zs[k], c)

    def y_dev(k):
        return dev(x, yo[k], z, c)

    def x_dev(k):
        return dev(xo[k], y, z, c)

    def blk_a(zz):
        return buf_a.at[zz, c]

    def blk_b(zz, yy):
        return buf_b.at[zz, c, yy]

    def blk_c(zz, xx):
        return buf_c.at[zz, c, xx]

    def z_blk(part, zz):
        return blk_a(zz) if part == "A" else blk_b(zz, y) if part == "B" else blk_c(zz, x)

    def slot_z(way, s, orient=1):
        return zs[-orient * s if way == "up" else orient * s]

    def hand_over(part, k, zz):
        if k in FINE:
            send(("core", part, k, 0), z_blk(part, zz), z_blk(part, zz), sibling)

    def last_blk(part, zz, k):
        return blk_b(zz, yo[k]) if part == "B" else blk_c(zz, xo[k])

    def ring_send(part, way, s):
        block = z_blk(part, slot_z(way, s - 1))
        send(("z", part, way, s), block, block, z_dev(1 if way == "up" else -1))

    def last_send(part, k, way):
        zz = slot_z(*SLOTS[k])
        block = last_blk(part, zz, -1 if way == "opp" else 0)
        there = y_dev if part == "B" else x_dev
        send(("last", part, k, way), block, block, there(-1 if way == "dn" else 1))

    def take_z(part, way, s):
        k = SLOT_OF[way, s]
        zz = slot_z(way, s)
        block = z_blk(part, zz)
        recv(("z", part, way, s), block, z_dev(-1 if way == "up" else 1))
        if part == "A":
            send(("core", "A", k), block, block, sibling)
        else:
            hand_over(part, k, zz)

    pieces_in = {}

    def take_last(part, k, way):
        zz = slot_z(*SLOTS[k])
        there = y_dev if part == "B" else x_dev
        block = last_blk(part, zz, {"up": -1, "dn": 1, "opp": 2}[way])
        recv(("last", part, k, way), block, there(1 if way == "dn" else -1))
        if k in FINE:
            send(("core", part, k, {"up": 1, "dn": 2, "opp": 3}[way]), block, block, sibling)
        else:
            pieces_in[part, k] = pieces_in.get((part, k), 0) + 1
            if pieces_in[part, k] == 3:
                whole = (buf_b if part == "B" else buf_c).at[zz, c]
                send(("core", part, k), whole, whole, sibling)

    def core_recv(k, zz):
        recv(("core", "A", k), buf_a.at[zz, sib], sibling)
        for part, ref, other in (("B", buf_b, yo), ("C", buf_c, xo)):
            if k in FINE:
                for piece, at in ((0, 0), (1, 1), (2, -1), (3, 2)):
                    recv(("core", part, k, piece), ref.at[zz, sib, other[at]], sibling)
            else:
                recv(("core", part, k), ref.at[zz, sib], sibling)

    def by_part(t):
        hi_t = t // NY
        yield slice(0, WA), slice(hi_t * WA, (hi_t + 1) * WA)
        for i in range(2):
            start = 2 * WA + (2 * i + hi_t) * WB
            yield slice(WA + i * WB, WA + (i + 1) * WB), slice(start, start + WB)

    def fill_head():
        for t in range(8):
            for source, place in by_part(t):
                columns = slice(t * FEAT + source.start, t * FEAT + source.stop)
                head[t % NY, :, place] = stage[:, columns].astype(BF16)

    def fill_right():
        for t in range(8):
            halves = [rt[half, t].astype(F32) for half in range(2)]
            for zz in range(NZ):
                rows = slice(8 * zz, 8 * zz + 8)
                both = jnp.concatenate([half[rows] for half in halves], axis=0).astype(BF16)
                for source, place in by_part(t):
                    slot_right[zz, t % NY, :, place] = both[:, source]

    offset = (pop * 8 + tp) * VOC

    def compute_one(zz):
        def tokens(piece, hi):
            return jnp.concatenate([piece(cc, hi * 2 + lo) for lo in range(2) for cc in range(2)], axis=0)

        def features(yy, carry):
            columns = [tokens(lambda cc, xx: buf_a[zz, cc, yy, xx], hi) for hi in range(2)]
            columns += [tokens(lambda cc, xx: buf_b[zz, cc, yy, xx], hi) for hi in range(2)]
            columns += [tokens(lambda cc, xx: buf_c[zz, cc, xx, yy], hi) for hi in range(2)]
            acc[...] += lax.dot_general(
                jnp.concatenate([head[yy], slot_right[zz, yy]], axis=0),
                jnp.concatenate(columns, axis=1), NT, preferred_element_type=F32,
            )
            return carry

        acc[...] = jnp.zeros((VOC + 16, 256), F32)
        lax.fori_loop(0, NY, features, 0)
        full = acc[...]
        lane = lax.broadcasted_iota(jnp.int32, (16, 256), 1)
        column = lax.broadcasted_iota(jnp.int32, (16, 256), 0)
        own = lax.shift_right_logical(column, 2) == lax.shift_right_logical(lane, 6)
        odd = lax.bitwise_and(lax.shift_right_logical(lane, 5), 1)
        sign = jnp.where(odd == 0, SIGMA_NOISE, -SIGMA_NOISE)
        few = jnp.where(own, full[VOC:] * sign, 0.0)
        spread = jnp.concatenate([few[:8]] * NZ + [few[8:]] * NZ, axis=0)
        place = lax.broadcasted_iota(jnp.int32, (FACT, 256), 0)
        here = lax.bitwise_and(lax.shift_right_logical(place, 3), NZ - 1) == zz
        lowrank = jnp.where(here, spread, 0.0).astype(BF16)
        logits = full[:VOC] + jnp.dot(left_ref[...], lowrank, preferred_element_type=F32)
        best = jnp.max(logits, axis=0, keepdims=True)
        total = jnp.sum(jnp.exp(logits - best), axis=0, keepdims=True)
        wanted = jnp.concatenate([tgt_ref[zz], tgt_ref[NZ + zz]], axis=1) - offset
        rows = lax.broadcasted_iota(jnp.int32, (VOC, 256), 0)
        target = jnp.sum(jnp.where(rows == wanted, logits, 0.0), axis=0, keepdims=True)
        packed = jnp.concatenate([best, total, target, jnp.zeros((5, 256), F32)], axis=0)
        st[zz, 0] = packed[:, :128]
        st[zz, 1] = packed[:, 128:]

    def stat_send(k):
        for i in range(2):
            if i or k:
                send(("stat1", i, k), st.at[zs[(k + 4) % 8], los[i]], r1.at[blk], dev(x_hi * 2 + los[i], y, zs[k], c))

    def compute(k):
        way, s = SLOTS[k]
        zz = slot_z(way, s, -1)
        core_recv(k, zz)
        compute_one(zz)
        stat_send(((8 - s if way == "dn" else s) + 4) % 8)

    def step(what, *which):
        if what == "snd":
            (ring_send if which[0] == "z" else last_send)(*which[1:])
        elif what == "z":
            take_z(*which)
        elif what == "y":
            take_last(*which)
        elif what == "comp":
            compute(*which)
        elif what == "head":
            for load in loads[3:]:
                load.wait()
            fill_head()
        elif what == "A2r":
            for d in (1, 3, 2):
                recv(("A2", d), buf_a.at[z, c, ys[-d]], plane(0, -d))
            send(("core", "A", 0), blk_a(z), blk_a(z), sibling)
        elif what == "Rtr":
            for d in range(1, 4):
                recv(("Rt", d), rt.at[c, x_hi * NY + ys[-d]], plane(0, -d))
            send(("Rx",), rt.at[c, pl.ds(x_hi * NY, NY)], rt.at[c, pl.ds(x_hi * NY, NY)], mirror)
        elif what == "Rxr":
            recv(("Rx",), rt.at[c, pl.ds((1 - x_hi) * NY, NY)], mirror)
            send(("Rd",), rt.at[c], rt.at[c], sibling)
        else:
            recv(("Rd",), rt.at[sib], sibling)
            fill_right()

    def follow(first, part):
        at = first
        while at < len(ORDER):
            action = ORDER[at]
            if part is not None and not (action[0] == "snd" and action[2] == part):
                break
            step(*action)
            at += 1
        return at

    for dx, dy in PLANE:
        recv(("sq", dx, dy), sq.at[xs[-dx], ys[-dy]], plane(-dx, -dy))
    scales = []
    for lo in range(2):
        total = sq[lo, :, 0, :] + sq[lo + 2, :, 0, :]
        row_scale = lax.rsqrt(jnp.sum(total, axis=0, keepdims=True) / D + NORM_EPS)
        scales.append(jnp.broadcast_to(row_scale, (128, 128)).T[:ROWS, :])
    own_scale = jnp.where(x_lo == 0, scales[0], scales[1])

    def normalize(values, scale, xx, yy, first, count):
        return jnp.concatenate(
            [
                (values[:, j * 128:(j + 1) * 128].astype(F32) * scale * sq[xx, yy, 1 + first + j:2 + first + j, :]).astype(BF16)
                for j in range(count)
            ],
            axis=1,
        )

    for d in (1, 3, 2):
        recv(("B1", d), raw_b.at[xs[-d]], plane(-d, 0))
    for t in range(NX):
        buf_b[z, c, y, t] = normalize(raw_b[t], scales[t % 2], t, y, 1, 2)
    hand_over("B", 0, z)
    start_from = follow(0, "B")
    for d in (1, 3, 2):
        recv(("C1", d), raw_c.at[ys[-d]], plane(0, -d))
    for t in range(NY):
        buf_c[z, c, x, t] = normalize(raw_c[t], own_scale, x, t, 3, 2)
    hand_over("C", 0, z)
    start_from = follow(start_from, "C")
    for d in (1, 3, 2):
        recv(("A1", d), raw_a.at[xs[-d]], plane(-d, 0))
    for t in range(NX):
        buf_a[z, c, y, t] = normalize(raw_a[t], scales[t % 2], t, y, 0, 1)
    for d in (1, 3, 2):
        send(("A2", d), buf_a.at[z, c, y], buf_a.at[z, c, y], plane(0, d))

    follow(start_from, None)

    r1[pl.ds(blk, 1)] = st[zs[4], x_lo][None]
    for copy in sent:
        copy.wait_send()
    sent.clear()
    for k in range(8):
        for i in range(2):
            if i or k:
                recv(("stat1", i, k), r1.at[los[i] * NZ + zs[-k if k < 5 else 8 - k]], dev(x_hi * 2 + los[i], y, zs[-k if k < 5 else 8 - k], c))
    best, total, target = combine(r1[...])
    packed = jnp.concatenate([best, total, target, jnp.zeros((5, 128), F32)], axis=0)
    r2[pl.ds(quad, 1)] = packed[None]

    def quad_at(i, k):
        h, d = divmod(k, 4)
        hi = x_hi if h == 0 else 1 - x_hi
        cc = c if i == 0 else sib
        return cc, hi, d

    QUAD = [(i, k) for i in (1, 0) for k in (6, 2, 5, 7, 1, 3, 4, 0) if i or k]
    RING = [(i, k) for i in (1, 0) for k in (4, 3, 5, 2, 6, 1, 7, 0) if i or k]
    for i, k in QUAD:
        cc, hi, d = quad_at(i, k)
        send(("stat2", i, k), r2.at[quad], r2.at[quad], dev(hi * 2 + x_lo, ys[d], z, cc))
    for i, k in QUAD:
        cc, hi, d = quad_at(i, k)
        recv(("stat2", i, k), r2.at[cc * 8 + hi * NY + ys[-d]], dev(hi * 2 + x_lo, ys[-d], z, cc))
    best, total, target = combine(r2[...])
    logprob = target - best - jnp.log(total)
    lane = lax.broadcasted_iota(jnp.int32, (1, 128), 1)
    zero = jnp.zeros((1, 128), F32)
    means = [
        jnp.sum(jnp.where(lax.shift_right_logical(lane, 5) == m, logprob, 0.0), axis=1, keepdims=True) / 32.0
        for m in range(4)
    ]
    loglik, weights = zero, zero
    owned = x_lo * NZ + zs[4]
    for m in range(4):
        loglik = jnp.where(lane == owned * 4 + m, means[m], loglik)
    for h in range(2):
        weights = jnp.where(lax.shift_right_logical(lane, 2) == owned * 2 + h, means[2 * h] - means[2 * h + 1], weights)
    packed = jnp.concatenate([loglik, weights, jnp.zeros((6, 128), F32)], axis=0)
    r3[pl.ds(blk, 1)] = packed[None]
    for i, k in RING:
        send(("stat3", i, k), r3.at[blk], r3.at[blk], dev(x_hi * 2 + los[i], y, zs[k], c))
    for i, k in RING:
        zz = zs[-k if k < 5 else 8 - k]
        recv(("stat3", i, k), r3.at[los[i] * NZ + zz], dev(x_hi * 2 + los[i], y, zz, c))
    out_ref[...] = jnp.sum(r3[...], axis=0)
    for copy in sent:
        copy.wait_send()


def update_kernel(w_ref, left_ref, rt_ref, master_ref, ll_ref, out_ref, block, sems):
    ll_ref[...] = w_ref[0, :64]
    scaled = (left_ref[...].astype(F32) * w_ref[1:2, :]).astype(BF16)
    copies = []
    for t in range(8):
        cols = slice(t * FEAT, (t + 1) * FEAT)
        right = jnp.concatenate([rt_ref[0, t], rt_ref[1, t]], axis=0)
        update = jnp.dot(scaled, right, preferred_element_type=F32)
        block[:, cols] = master_ref[:, cols] + LEARN_RATE * update
        copy = pltpu.make_async_copy(block.at[:, cols], out_ref.at[:, cols], sems.at[t])
        copy.start()
        copies.append(copy)
    for copy in copies:
        copy.wait()


def body(hidden, norm_gain, right_factors, left_factors, targets, master):
    vmem = pl.BlockSpec(memory_space=pltpu.VMEM)
    hbm = pl.BlockSpec(memory_space=pl.ANY)
    result, stage, right_t = pl.pallas_call(
        gather_kernel,
        out_shape=(
            pltpu.VMEM((8, 128), F32),
            pltpu.VMEM((VOC, D), F32),
            pltpu.VMEM((2, 8, 64, FEAT), BF16),
        ),
        in_specs=[hbm] * 6,
        out_specs=(vmem, vmem, vmem),
        scratch_shapes=[
            pltpu.VMEM((ROWS, FEAT), BF16),
            pltpu.VMEM((FEAT,), F32),
            pltpu.VMEM((FEAT, FACT), BF16),
            pltpu.VMEM((VOC, FACT), BF16),
            pltpu.VMEM((16, 1, 128), jnp.int32),
            pltpu.VMEM((NZ, 2, NY, NX, ROWS, WA), BF16),
            pltpu.VMEM((NZ, 2, NY, NX, ROWS, WB), BF16),
            pltpu.VMEM((NZ, 2, NX, NY, ROWS, WB), BF16),
            pltpu.VMEM((NY, VOC, 2 * FEAT), BF16),
            pltpu.VMEM((NZ, NY, 16, 2 * FEAT), BF16),
            pltpu.VMEM((VOC + 16, 256), F32),
            pltpu.VMEM((NX, ROWS, WA), BF16),
            pltpu.VMEM((NX, ROWS, WB), BF16),
            pltpu.VMEM((NY, ROWS, WB), BF16),
            pltpu.VMEM((NX, NY, 8, 128), F32),
            pltpu.VMEM((NZ, 2, 8, 128), F32),
            pltpu.VMEM((16, 8, 128), F32),
            pltpu.VMEM((16, 8, 128), F32),
            pltpu.VMEM((16, 8, 128), F32),
            pltpu.SemaphoreType.DMA((N_MSG,)),
            pltpu.SemaphoreType.DMA((N_MSG,)),
            pltpu.SemaphoreType.DMA((6,)),
        ],
        compiler_params=pltpu.CompilerParams(
            collective_id=0, has_side_effects=True, vmem_limit_bytes=52 * 1024 * 1024
        ),
        name="gather_logits",
    )(
        hidden, norm_gain, right_factors, left_factors,
        targets.reshape(16, 1, 128), master,
    )
    loglik, new_master = pl.pallas_call(
        update_kernel,
        out_shape=(jax.ShapeDtypeStruct((64,), F32), jax.ShapeDtypeStruct((VOC, D), F32)),
        in_specs=[vmem, vmem, vmem, vmem],
        out_specs=(vmem, hbm),
        scratch_shapes=[pltpu.VMEM((VOC, D), F32), pltpu.SemaphoreType.DMA((8,))],
        compiler_params=pltpu.CompilerParams(vmem_limit_bytes=20 * 1024 * 1024),
        name="update_master",
    )(result, left_factors, right_t, stage)
    return (loglik, new_master)


def solution(mesh):
    in_specs = (
        P("pop", "tp"),
        P("tp"),
        P("tp", None),
        P(("pop", "tp"), None),
        P(),
        P(("pop", "tp"), None),
    )
    out_specs = (P(), P(("pop", "tp"), None))
    return jax.shard_map(body, mesh=mesh, in_specs=in_specs, out_specs=out_specs, check_vma=False)
```
